32 devices in a mesh: groups: 2 (over x), tm: 16 (over z, y, core).
Axes of the slice: x: 2, y: 2, z: 4, core: 2. Of those that a mesh axis runs over, the one named last changes fastest.
Arguments:
- latents: bfloat16 [2048, 2, 32, 256], P(('groups', 'tm')), parts along dimension 0, may hold values from -6 to 6
- input_map: bfloat16 [9, 256, 256], replicated, may hold values from -0.125 to 0.125
- output_map: bfloat16 [9, 256, 256], replicated, may hold values from -0.03125 to 0.03125
- decay_rate: float32 [256], replicated, may hold values from 0 to 1
- frame_step: float32 [2048], P(('groups', 'tm')), parts along dimension 0, may hold values from 0.6 to 512
- cotangent: bfloat16 [2048, 2, 32, 256], P(('groups', 'tm')), parts along dimension 0, may hold values from -6 to 6
Outputs:
- layer_out: bfloat16 [2048, 2, 32, 256], P(('groups', 'tm')), parts along dimension 0
- grad_latents: bfloat16 [2048, 2, 32, 256], P(('groups', 'tm')), parts along dimension 0
- grad_input_map: float32 [18, 256, 256], P('groups'), parts along dimension 0
- grad_output_map: float32 [18, 256, 256], P('groups'), parts along dimension 0
- grad_log_rate: float32 [512], P('groups'), parts along dimension 0
The draws below stay inside these ranges and needn't reach their ends.
There are 2 independent parts, one for each index of `groups`. The reference program is written for one: setup_inputs(seed, part) draws one part's arguments, and reference() takes and returns one part's arrays. A program takes and returns all parts, laid end to end along the dimension named above; an argument that names none is the same for every part. Nothing has to cross between parts.
All inputs are finite; a program needn't handle non-finite values.
Results may differ from the reference program's by a relative error of at most 0.005.
Values sent between devices are 32-bit elements; how exact they have to be, the bound alone decides.
No kernel may reach another device: no remote copies, remote signals or barrier semaphores. Data moves between devices by JAX's collectives and lax.ppermute only.
A program may use at most 192 MiB of HBM per device.

```python
import math
import jax
import jax.numpy as jnp
from jax import lax

P_SIZE = 256
N = 256
ROWS = 2
W = 32
FRAMES = 1024


def draw_decay_rate(key, part):
    unit = jax.random.uniform(key, (N,), jnp.float32)
    lowest = math.log(0.3 / FRAMES)
    highest = math.log(0.15)
    return jnp.exp(lowest + (highest - lowest) * unit)


def draw_frame_step(key, part):
    base_key, first_key, gap_key, amount_key = jax.random.split(key, 4)
    base = jax.random.uniform(base_key, (FRAMES,), jnp.float32, 0.6, 1.4)
    first = jax.random.randint(first_key, (), 0, FRAMES)
    gap = jax.random.randint(gap_key, (), 1, FRAMES)
    second = (first + gap) % FRAMES
    half = float(FRAMES // 2)
    other = jax.random.uniform(amount_key, (), jnp.float32, 0.25, 0.5) * half * 2.0
    other = jnp.minimum(other, half)
    positions = jnp.arange(FRAMES)
    result = jnp.where(positions == first, half, base)
    result = jnp.where(positions == second, other, result)
    return result


def steps_of(stream_key, extent, shards, low, largest):
    level = 1.0
    for dim, parts in shards:
        heights = jax.random.uniform(jax.random.fold_in(jax.random.fold_in(stream_key, 6), dim), (parts,), jnp.float32, low / len(shards), largest / len(shards))
        level = level * jnp.repeat(jnp.exp(heights), extent[dim] // parts).reshape((-1,) + (1,) * (len(extent) - 1 - dim))
    return level


def centred(key, shape, scale, most, shards=(), dtype=jnp.bfloat16):
    values = scale * jax.random.normal(key, shape, jnp.float32)
    if shards:
        values = values * steps_of(key, shape, shards, -0.22, 0.18)
    return jnp.clip(values, -most, most).astype(dtype)


def setup_inputs(seed: int = 0, part: int = 0) -> dict:
    splits = jax.random.split(jax.random.key(seed), 7)
    own_keys = jax.random.split(jax.random.fold_in(splits[6], part), 7)
    return {
        "latents": centred(own_keys[0], (FRAMES, ROWS, W, P_SIZE), 1.0, 6.0, ((0, 16),)),
        "input_map": centred(splits[1], (9, P_SIZE, N), (9 * P_SIZE) ** -0.5, 0.125),
        "output_map": centred(splits[2], (9, N, P_SIZE), (144 * N) ** -0.5, 0.03125),
        "decay_rate": draw_decay_rate(jax.random.fold_in(splits[6], 71), part),
        "frame_step": draw_frame_step(jax.random.fold_in(jax.random.fold_in(splits[6], part), 71), part),
        "cotangent": centred(own_keys[5], (FRAMES, ROWS, W, P_SIZE), 1.0, 6.0, ((0, 16),)),
    }


def conv_same(source, kernel):
    height, breadth = (source.shape[1], source.shape[2])
    padded = jnp.pad(source, ((0, 0), (1, 1), (1, 1), (0, 0)))
    total = jnp.zeros(source.shape[:3] + (kernel.shape[2],), jnp.float32)
    for offset in range(9):
        window = padded[:, offset // 3:offset // 3 + height, offset % 3:offset % 3 + breadth, :]
        total = total + lax.dot_general(window, kernel[offset], (((3,), (0,)), ((), ())), preferred_element_type=jnp.float32)
    return total

def kernel_grad(source, target):
    height, breadth = (source.shape[1], source.shape[2])
    padded = jnp.pad(source, ((0, 0), (1, 1), (1, 1), (0, 0)))
    pieces = []
    for offset in range(9):
        window = padded[:, offset // 3:offset // 3 + height, offset % 3:offset % 3 + breadth, :]
        pieces.append(lax.dot_general(window, target, (((0, 1, 2), (0, 1, 2)), ((), ())), preferred_element_type=jnp.float32))
    return jnp.stack(pieces)

def flipped(kernel):
    return jnp.transpose(kernel[::-1], (0, 2, 1))

def forward_step(previous, inputs):
    factor_now, driven_now = inputs
    updated = factor_now[None, None, :] * previous + driven_now
    return (updated, updated)

def reference(latents, input_map, output_map, decay_rate, frame_step, cotangent):
    driven = conv_same(latents, input_map)
    decays = jnp.exp(-frame_step[:, None] * decay_rate[None, :])
    blank_map = jnp.zeros(driven.shape[1:], jnp.float32)
    _, states = lax.scan(forward_step, blank_map, (decays, driven))
    states_low = states.astype(jnp.bfloat16)
    layer_out = conv_same(states_low, output_map).astype(jnp.bfloat16)
    pulled = conv_same(cotangent, flipped(output_map))
    decays_next = jnp.concatenate([decays[1:], jnp.zeros((1, decays.shape[1]), jnp.float32)], axis=0)
    _, adjoint = lax.scan(forward_step, blank_map, (decays_next, pulled), reverse=True)
    adjoint_low = adjoint.astype(jnp.bfloat16)
    grad_latents = conv_same(adjoint_low, flipped(input_map)).astype(jnp.bfloat16)
    factor = 1.0 / math.sqrt(FRAMES * ROWS * W)
    grad_input_map = kernel_grad(latents, adjoint_low) * factor
    grad_output_map = kernel_grad(states_low, cotangent) * factor
    states_before = jnp.concatenate([blank_map[None], states[:-1]], axis=0)
    weighted = lax.optimization_barrier(jnp.sum(adjoint * states_before, axis=(1, 2)))
    grad_log_rate = -factor * decay_rate * lax.optimization_barrier(jnp.sum(frame_step[:, None] * decays * weighted, axis=0))
    return (layer_out, grad_latents, grad_input_map, grad_output_map, grad_log_rate)
```

```python
import functools
import math

import jax
import jax.numpy as jnp
from jax import lax
from jax.experimental import pallas as pl
from jax.experimental.pallas import tpu as pltpu
from jax.sharding import PartitionSpec as P

F32 = jnp.float32
BF16 = jnp.bfloat16
EXTRA = 8
VMEM_LIMIT = 40 * 1024 * 1024


def column_shifts(value):
    frames, height, breadth, channels = value.shape
    rows = frames * height * breadth
    flat = value.reshape(rows, channels).astype(F32)
    column = lax.broadcasted_iota(jnp.int32, (rows, channels), 0) % breadth
    before = jnp.where(column == 0, 0.0, pltpu.roll(flat, 1, 0)).astype(BF16)
    after = jnp.where(column == breadth - 1, 0.0, pltpu.roll(flat, rows - 1, 0)).astype(BF16)
    return before.reshape(value.shape), value, after.reshape(value.shape)


def conv_rows(value, weights):
    frames, _, breadth, channels = value.shape
    shifted = column_shifts(value)
    pieces = [piece[:, row].reshape(frames * breadth, channels) for row in (0, 1) for piece in shifted]
    patches = jnp.concatenate(pieces, axis=1)
    outs = []
    for first in (3, 0):
        taps = weights[first : first + 6].reshape(6 * channels, weights.shape[2])
        outs.append(jnp.dot(patches, taps, preferred_element_type=F32))
    return outs


def flip_into(flipped_ref, weights_ref):
    for tap in range(9):
        flipped_ref[tap] = weights_ref[8 - tap].T


def decay_of(step, rate):
    return jnp.exp(-(step * rate))


def drive_kernel(reverse, step_ref, rate_ref, value_ref, weights_ref, driven_ref, carry_ref, state, decay, flipped):
    index, count = pl.program_id(0), pl.num_programs(0)
    block, _, breadth, channels = driven_ref.shape

    @pl.when(index == 0)
    def _():
        state[...] = jnp.zeros_like(state)
        decay[...] = jnp.ones_like(decay)
        if reverse:
            flip_into(flipped, weights_ref)

    outs = conv_rows(value_ref[...], flipped if reverse else weights_ref)
    for row, out in enumerate(outs):
        driven_ref[:, row] = out.reshape(block, breadth, channels)
    first = (count - 1 - index if reverse else index) * block
    rate = jnp.broadcast_to(rate_ref[...], decay.shape)
    total, held = decay[...], state[...]
    for offset in range(block):
        frame = block - 1 - offset if reverse else offset
        factor = decay_of(step_ref[first + frame], rate)
        driven = driven_ref[frame].reshape(state.shape)
        held = factor[None] * (held + driven) if reverse else factor[None] * held + driven
        total = total * factor
    state[...] = held
    decay[...] = total

    @pl.when(index == count - 1)
    def _():
        rows = state.shape[0] * 8
        carry_ref[:rows] = held.reshape(rows, channels)
        carry_ref[rows:] = total


def add_kernel_grad(sums, source, target):
    frames, height, breadth, channels = source.shape
    before, same, after = column_shifts(target)
    taps = jnp.concatenate([after, same, before], axis=-1)

    def contract(left, right):
        return lax.dot_general(
            left.reshape(-1, channels), right.reshape(-1, 3 * channels), (((0,), (0,)), ((), ())), preferred_element_type=F32
        )

    sums[1] += contract(source, taps)
    sums[0] += contract(source[:, 0], taps[:, 1])
    sums[2] += contract(source[:, 1], taps[:, 0])


def split_grad(scale, sums, whole, core, keep_ref, send_ref):
    channels = sums.shape[1]
    for tap in range(9):
        piece = sums[tap // 3, :, (tap % 3) * channels : (tap % 3 + 1) * channels]
        whole[tap * channels : (tap + 1) * channels] = piece * scale
    half = whole.shape[0] // 2
    keep_ref[:half] = whole[pl.ds(core * half, half)]
    send_ref[:half] = whole[pl.ds((1 - core) * half, half)]


def state_kernel(
    scale, step_ref, core_ref, rate_ref, incoming_ref, driven_ref, cotangent_ref, low_ref, keep_ref, send_ref, state, sums, whole
):
    index, count = pl.program_id(0), pl.num_programs(0)
    block = driven_ref.shape[0]

    @pl.when(index == 0)
    def _():
        state[...] = incoming_ref[...].reshape(state.shape)
        sums[...] = jnp.zeros_like(sums)

    rate = jnp.broadcast_to(rate_ref[...], (8, rate_ref.shape[1]))
    held = state[...]
    for frame in range(block):
        factor = decay_of(step_ref[index * block + frame], rate)
        held = factor[None] * held + driven_ref[frame].reshape(state.shape)
        low_ref[frame] = held.astype(BF16).reshape(low_ref.shape[1:])
    state[...] = held
    add_kernel_grad(sums, low_ref[...], cotangent_ref[...])

    @pl.when(index == count - 1)
    def _():
        split_grad(scale, sums, whole, core_ref[0], keep_ref, send_ref)


def adjoint_kernel(
    scale,
    step_ref,
    core_ref,
    rate_ref,
    arriving_ref,
    incoming_ref,
    pulled_ref,
    latents_ref,
    states_ref,
    previous_ref,
    low_ref,
    keep_ref,
    send_ref,
    carry,
    rate_sum,
    sums,
    whole,
):
    index, count = pl.program_id(0), pl.num_programs(0)
    block = pulled_ref.shape[0]
    first = (count - 1 - index) * block

    @pl.when(index == 0)
    def _():
        carry[...] = arriving_ref[...].reshape(carry.shape)
        rate_sum[...] = jnp.zeros_like(rate_sum)
        sums[...] = jnp.zeros_like(sums)

    rate = jnp.broadcast_to(rate_ref[...], rate_sum.shape)
    held, summed = carry[...], rate_sum[...]
    for frame in range(block - 1, -1, -1):
        step = step_ref[first + frame]
        adjoint = held + pulled_ref[frame].reshape(carry.shape)
        low_ref[frame] = adjoint.astype(BF16).reshape(low_ref.shape[1:])
        held = decay_of(step, rate)[None] * adjoint
        if frame:
            before = states_ref[frame - 1].astype(F32).reshape(carry.shape)
        else:
            before = jnp.where(
                index == count - 1,
                incoming_ref[...].reshape(carry.shape),
                previous_ref[0].astype(F32).reshape(carry.shape),
            )
        summed = summed + step * jnp.sum(held * before, axis=0)
    carry[...] = held
    rate_sum[...] = summed
    add_kernel_grad(sums, latents_ref[...], low_ref[...])

    @pl.when(index == count - 1)
    def _():
        split_grad(scale, sums, whole, core_ref[0], keep_ref, send_ref)
        half = whole.shape[0] // 2
        keep_ref[half:] = summed
        send_ref[half:] = summed


def conv_kernel(reverse, value_ref, weights_ref, out_ref, flipped):
    if reverse:

        @pl.when(pl.program_id(0) == 0)
        def _():
            flip_into(flipped, weights_ref)

    block, _, breadth, channels = out_ref.shape
    outs = conv_rows(value_ref[...], flipped if reverse else weights_ref)
    for row, out in enumerate(outs):
        out_ref[:, row] = out.astype(BF16).reshape(block, breadth, channels)


def call(kernel, grid, in_specs, out_specs, out_shape, scratch, flops, moved, name):
    return pl.pallas_call(
        kernel,
        grid=grid,
        in_specs=in_specs,
        out_specs=out_specs,
        out_shape=out_shape,
        scratch_shapes=scratch,
        compiler_params=pltpu.CompilerParams(vmem_limit_bytes=VMEM_LIMIT, dimension_semantics=("arbitrary",) * len(grid)),
        cost_estimate=pl.CostEstimate(flops=flops, bytes_accessed=moved, transcendentals=0),
        name=name,
    )


def smem():
    return pl.BlockSpec(memory_space=pltpu.SMEM)


def fixed(shape):
    return pl.BlockSpec(shape, lambda g: (0,) * len(shape))


def framed(shape, block, count, reverse):
    return pl.BlockSpec((block,) + shape[1:], lambda g: ((count - 1 - g if reverse else g), 0, 0, 0))


def fold(bit, keep, recv, main, last):
    rows, columns = keep.shape
    extra = rows - main
    half = main if last else main // 2

    def kernel(bit_ref, keep_ref, recv_ref, *outs):
        if last:
            outs[0][...] = keep_ref[...] + recv_ref[...]
            return
        for out, part in zip(outs, (bit_ref[0], 1 - bit_ref[0])):
            window = pl.ds(part * half, half)
            out[:half] = keep_ref[window] + recv_ref[window]
            if extra:
                out[half:] = keep_ref[main:] + recv_ref[main:]

    shape = jax.ShapeDtypeStruct((half + extra, columns), F32)
    outs = [shape] if last else [shape, shape]
    whole = pl.BlockSpec(memory_space=pltpu.VMEM)
    return pl.pallas_call(
        kernel,
        in_specs=[smem(), whole, whole],
        out_specs=[whole] * len(outs),
        out_shape=outs,
        cost_estimate=pl.CostEstimate(flops=rows * columns, bytes_accessed=12 * rows * columns, transcendentals=0),
        name="fold",
    )(bit, keep, recv)


def merge(bit, mine, other):
    rows, columns = mine.shape

    def kernel(bit_ref, mine_ref, other_ref, out_ref):
        out_ref[pl.ds(bit_ref[0] * rows, rows)] = mine_ref[...]
        out_ref[pl.ds((1 - bit_ref[0]) * rows, rows)] = other_ref[...]

    whole = pl.BlockSpec(memory_space=pltpu.VMEM)
    return pl.pallas_call(
        kernel,
        in_specs=[smem(), whole, whole],
        out_specs=whole,
        out_shape=jax.ShapeDtypeStruct((2 * rows, columns), F32),
        cost_estimate=pl.CostEstimate(flops=0, bytes_accessed=16 * rows * columns, transcendentals=0),
        name="merge",
    )(bit, mine, other)


def swap(value, count, distance):
    return lax.ppermute(value, "tm", [(source, source ^ distance) for source in range(count)])


def bits_of(me, levels):
    return [jnp.bitwise_and(lax.shift_right_logical(me, level), 1).reshape(1) for level in range(levels)]


def sum_over(keep, send, main, bits, count):
    levels = len(bits)
    for level in range(levels):
        recv = swap(send, count, 1 << level)
        last = level == levels - 1
        if last:
            (keep,) = fold(bits[level], keep, recv, main, True)
        else:
            keep, send = fold(bits[level + 1], keep, recv, main, False)
            main = main // 2
    extra = keep[main:]
    piece = keep[:main]
    for level in range(levels - 1, -1, -1):
        piece = merge(bits[level], piece, swap(piece, count, 1 << level))
    return piece, extra


def carry_in(carry, bits, count, reverse):
    rows = carry.shape[0] - 8
    local, decay = carry[:rows].reshape(rows // 8, 8, -1), carry[rows:][None]
    reached, passed = jnp.zeros_like(local), jnp.ones_like(decay)
    levels = len(bits)
    for level in range(levels):
        distance = 1 << level
        message = jnp.concatenate([local.reshape(rows, -1), decay[0]], axis=0)
        if level < levels - 1:
            other = swap(message, count, distance)
        else:
            towards = 0 if reverse else distance
            pairs = [(source, source ^ distance) for source in range(count) if (source ^ distance) & distance == towards]
            other = lax.ppermute(message, "tm", pairs)
        other_local, other_decay = other[:rows].reshape(rows // 8, 8, -1), other[rows:][None]
        later = bits[level][0] == (0 if reverse else 1)
        reached = jnp.where(later, reached + passed * other_local, reached)
        passed = jnp.where(later, passed * other_decay, passed)
        local = jnp.where(later, decay * other_local + local, other_decay * local + other_local)
        decay = decay * other_decay
    return reached.reshape(rows, -1)


def body(latents, input_map, output_map, decay_rate, frame_step, cotangent):
    frames, height, breadth, channels = latents.shape
    count = lax.axis_size("tm")
    levels = count.bit_length() - 1
    me = lax.axis_index("tm")
    bits = bits_of(me, levels)
    factor = 1.0 / math.sqrt(frames * count * height * breadth)
    block = 16
    steps = frames // block
    grid = (steps,)
    rate = decay_rate.reshape(1, channels)
    map_rows = height * breadth
    shape = latents.shape
    weights = input_map.shape
    pixels = frames * height * breadth
    flops = 2 * pixels * 6 * channels * channels
    driven_type = jax.ShapeDtypeStruct(shape, F32)
    low_type = jax.ShapeDtypeStruct(shape, BF16)
    map_scratch = pltpu.VMEM((map_rows // 8, 8, channels), F32)
    decay_scratch = pltpu.VMEM((8, channels), F32)
    flip_scratch = pltpu.VMEM(weights, BF16)

    def drive(value, kernel_map, reverse):
        return call(
            functools.partial(drive_kernel, reverse),
            grid,
            [smem(), fixed(rate.shape), framed(shape, block, steps, reverse), fixed(weights)],
            [framed(shape, block, steps, reverse), fixed((map_rows + 8, channels))],
            [driven_type, jax.ShapeDtypeStruct((map_rows + 8, channels), F32)],
            [map_scratch, decay_scratch, flip_scratch],
            flops,
            pixels * channels * 6,
            "pull" if reverse else "drive",
        )(frame_step, rate, value, kernel_map)

    driven, forward_carry = drive(latents, input_map, False)
    pulled, backward_carry = drive(cotangent, output_map, True)
    incoming = carry_in(forward_carry, bits, count, False)
    arriving = carry_in(backward_carry, bits, count, True)

    grad_rows = 9 * channels
    half = grad_rows // 2
    sums_scratch = pltpu.VMEM((3, channels, 3 * channels), F32)
    whole_scratch = pltpu.VMEM((grad_rows, channels), F32)
    half_type = jax.ShapeDtypeStruct((half, channels), F32)
    half_extra = jax.ShapeDtypeStruct((half + EXTRA, channels), F32)

    states_low, out_keep, out_send = call(
        functools.partial(state_kernel, factor),
        grid,
        [
            smem(),
            smem(),
            fixed(rate.shape),
            fixed(incoming.shape),
            framed(shape, block, steps, False),
            framed(shape, block, steps, False),
        ],
        [framed(shape, block, steps, False), fixed(half_type.shape), fixed(half_type.shape)],
        [low_type, half_type, half_type],
        [map_scratch, sums_scratch, whole_scratch],
        flops,
        pixels * channels * 8,
        "states",
    )(frame_step, bits[0], rate, incoming, driven, cotangent)

    adjoint_low, in_keep, in_send = call(
        functools.partial(adjoint_kernel, factor),
        grid,
        [
            smem(),
            smem(),
            fixed(rate.shape),
            fixed(incoming.shape),
            fixed(incoming.shape),
            framed(shape, block, steps, True),
            framed(shape, block, steps, True),
            framed(shape, block, steps, True),
            pl.BlockSpec((1,) + shape[1:], lambda g: (jnp.maximum((steps - 1 - g) * block - 1, 0), 0, 0, 0)),
        ],
        [framed(shape, block, steps, True), fixed(half_extra.shape), fixed(half_extra.shape)],
        [low_type, half_extra, half_extra],
        [map_scratch, decay_scratch, sums_scratch, whole_scratch],
        flops,
        pixels * channels * 10,
        "adjoint",
    )(frame_step, bits[0], rate, arriving, incoming, pulled, latents, states_low, states_low)

    def conv(value, kernel_map, reverse):
        return call(
            functools.partial(conv_kernel, reverse),
            grid,
            [framed(shape, block, steps, False), fixed(weights)],
            framed(shape, block, steps, False),
            low_type,
            [flip_scratch],
            flops,
            pixels * channels * 4,
            "conv",
        )(value, kernel_map)

    layer_out = conv(states_low, output_map, False)
    grad_latents = conv(adjoint_low, input_map, True)
    grad_output_map, _ = sum_over(out_keep, out_send, half, bits, count)
    grad_input_map, rate_rows = sum_over(in_keep, in_send, half, bits, count)
    grad_log_rate = -factor * decay_rate * jnp.sum(rate_rows, axis=0)
    return (
        layer_out,
        grad_latents,
        grad_input_map.reshape(weights),
        grad_output_map.reshape(weights),
        grad_log_rate,
    )


def solution(mesh):
    in_specs = (
        P(("groups", "tm"), None, None, None),
        P(),
        P(),
        P(),
        P(("groups", "tm")),
        P(("groups", "tm"), None, None, None),
    )
    out_specs = (
        P(("groups", "tm"), None, None, None),
        P(("groups", "tm"), None, None, None),
        P("groups", None, None),
        P("groups", None, None),
        P("groups"),
    )
    return jax.shard_map(body, mesh=mesh, in_specs=in_specs, out_specs=out_specs, check_vma=False)
```

```python
import functools
import math

import jax
import jax.numpy as jnp
from jax import lax
from jax.experimental import pallas as pl
from jax.experimental.pallas import tpu as pltpu
from jax.sharding import PartitionSpec as P

F32 = jnp.float32
BF16 = jnp.bfloat16
EXTRA = 8
VMEM_LIMIT = 20 * 1024 * 1024


def column_shifts(value):
    frames, height, breadth, channels = value.shape
    rows = frames * height * breadth
    flat = value.reshape(rows, channels).astype(F32)
    column = lax.broadcasted_iota(jnp.int32, (rows, channels), 0) % breadth
    before = jnp.where(column == 0, 0.0, pltpu.roll(flat, 1, 0)).astype(BF16)
    after = jnp.where(column == breadth - 1, 0.0, pltpu.roll(flat, rows - 1, 0)).astype(BF16)
    return before.reshape(value.shape), value, after.reshape(value.shape)


def conv_rows(value, weights):
    frames, _, breadth, channels = value.shape
    shifted = column_shifts(value)
    pieces = [piece[:, row].reshape(frames * breadth, channels) for row in (0, 1) for piece in shifted]
    patches = jnp.concatenate(pieces, axis=1)
    outs = []
    for first in (3, 0):
        taps = weights[first : first + 6].reshape(6 * channels, weights.shape[2])
        outs.append(jnp.dot(patches, taps, preferred_element_type=F32))
    return outs


def flip_into(flipped_ref, weights_ref):
    for tap in range(9):
        flipped_ref[tap] = weights_ref[8 - tap].T


def decay_of(step, rate):
    return jnp.exp(-(step * rate))


def drive_kernel(reverse, base, fresh, step_ref, rate_ref, value_ref, weights_ref, *refs):
    start_ref, refs = (None, refs) if fresh else (refs[0], refs[1:])
    driven_ref, carry_ref, state, decay, flipped = refs
    index, count = pl.program_id(0), pl.num_programs(0)
    block, _, breadth, channels = driven_ref.shape
    map_rows = state.shape[0] * 8

    @pl.when(index == 0)
    def _():
        state[...] = jnp.zeros_like(state) if fresh else start_ref[:map_rows].reshape(state.shape)
        decay[...] = jnp.ones_like(decay) if fresh else start_ref[map_rows:]
        if reverse:
            flip_into(flipped, weights_ref)

    outs = conv_rows(value_ref[...], flipped if reverse else weights_ref)
    for row, out in enumerate(outs):
        driven_ref[:, row] = out.reshape(block, breadth, channels)
    first = (base + (count - 1 - index if reverse else index)) * block
    rate = jnp.broadcast_to(rate_ref[...], decay.shape)
    total, held = decay[...], state[...]
    for offset in range(block):
        frame = block - 1 - offset if reverse else offset
        factor = decay_of(step_ref[first + frame], rate)
        driven = driven_ref[frame].reshape(state.shape)
        held = factor[None] * (held + driven) if reverse else factor[None] * held + driven
        total = total * factor
    state[...] = held
    decay[...] = total

    @pl.when(index == count - 1)
    def _():
        carry_ref[:map_rows] = held.reshape(map_rows, channels)
        carry_ref[map_rows:] = total


def add_kernel_grad(sums, source, target):
    frames, height, breadth, channels = source.shape
    before, same, after = column_shifts(target)
    taps = jnp.concatenate([after, same, before], axis=-1)

    def contract(left, right):
        return lax.dot_general(
            left.reshape(-1, channels), right.reshape(-1, 3 * channels), (((0,), (0,)), ((), ())), preferred_element_type=F32
        )

    sums[1] += contract(source, taps)
    sums[0] += contract(source[:, 0], taps[:, 1])
    sums[2] += contract(source[:, 1], taps[:, 0])


def split_grad(scale, sums, whole, core, keep_ref, send_ref):
    channels = sums.shape[1]
    for tap in range(9):
        piece = sums[tap // 3, :, (tap % 3) * channels : (tap % 3 + 1) * channels]
        whole[tap * channels : (tap + 1) * channels] = piece * scale
    half = whole.shape[0] // 2
    keep_ref[:half] = whole[pl.ds(core * half, half)]
    send_ref[:half] = whole[pl.ds((1 - core) * half, half)]


def state_kernel(
    scale, step_ref, core_ref, rate_ref, incoming_ref, driven_ref, cotangent_ref, low_ref, keep_ref, send_ref, state, sums, whole
):
    index, count = pl.program_id(0), pl.num_programs(0)
    block = driven_ref.shape[0]

    @pl.when(index == 0)
    def _():
        state[...] = incoming_ref[...].reshape(state.shape)
        sums[...] = jnp.zeros_like(sums)

    rate = jnp.broadcast_to(rate_ref[...], (8, rate_ref.shape[1]))
    held = state[...]
    for frame in range(block):
        factor = decay_of(step_ref[index * block + frame], rate)
        held = factor[None] * held + driven_ref[frame].reshape(state.shape)
        low_ref[frame] = held.astype(BF16).reshape(low_ref.shape[1:])
    state[...] = held
    add_kernel_grad(sums, low_ref[...], cotangent_ref[...])

    @pl.when(index == count - 1)
    def _():
        split_grad(scale, sums, whole, core_ref[0], keep_ref, send_ref)


def adjoint_kernel(
    scale,
    late_steps,
    step_ref,
    core_ref,
    rate_ref,
    arriving_ref,
    incoming_ref,
    late_ref,
    early_ref,
    latents_ref,
    states_ref,
    previous_ref,
    low_ref,
    keep_ref,
    send_ref,
    carry,
    rate_sum,
    sums,
    whole,
):
    index, count = pl.program_id(0), pl.num_programs(0)
    block = late_ref.shape[0]
    first = (count - 1 - index) * block

    @pl.when(index == 0)
    def _():
        carry[...] = arriving_ref[...].reshape(carry.shape)
        rate_sum[...] = jnp.zeros_like(rate_sum)
        sums[...] = jnp.zeros_like(sums)

    rate = jnp.broadcast_to(rate_ref[...], rate_sum.shape)
    held, summed = carry[...], rate_sum[...]
    for frame in range(block - 1, -1, -1):
        step = step_ref[first + frame]
        pulled = jnp.where(index < late_steps, late_ref[frame], early_ref[frame])
        adjoint = held + pulled.reshape(carry.shape)
        low_ref[frame] = adjoint.astype(BF16).reshape(low_ref.shape[1:])
        held = decay_of(step, rate)[None] * adjoint
        if frame:
            before = states_ref[frame - 1].astype(F32).reshape(carry.shape)
        else:
            before = jnp.where(
                index == count - 1,
                incoming_ref[...].reshape(carry.shape),
                previous_ref[0].astype(F32).reshape(carry.shape),
            )
        summed = summed + step * jnp.sum(held * before, axis=0)
    carry[...] = held
    rate_sum[...] = summed
    add_kernel_grad(sums, latents_ref[...], low_ref[...])

    @pl.when(index == count - 1)
    def _():
        split_grad(scale, sums, whole, core_ref[0], keep_ref, send_ref)
        half = whole.shape[0] // 2
        keep_ref[half:] = summed
        send_ref[half:] = summed


def conv_kernel(reverse, value_ref, weights_ref, out_ref, flipped):
    if reverse:

        @pl.when(pl.program_id(0) == 0)
        def _():
            flip_into(flipped, weights_ref)

    block, _, breadth, channels = out_ref.shape
    outs = conv_rows(value_ref[...], flipped if reverse else weights_ref)
    for row, out in enumerate(outs):
        out_ref[:, row] = out.astype(BF16).reshape(block, breadth, channels)


def call(kernel, grid, in_specs, out_specs, out_shape, scratch, flops, moved, name):
    return pl.pallas_call(
        kernel,
        grid=grid,
        in_specs=in_specs,
        out_specs=out_specs,
        out_shape=out_shape,
        scratch_shapes=scratch,
        compiler_params=pltpu.CompilerParams(vmem_limit_bytes=VMEM_LIMIT, dimension_semantics=("arbitrary",) * len(grid)),
        cost_estimate=pl.CostEstimate(flops=flops, bytes_accessed=moved, transcendentals=0),
        name=name,
    )


def far(value):
    return pltpu.with_memory_space_constraint(value, pltpu.HBM)


def smem():
    return pl.BlockSpec(memory_space=pltpu.SMEM)


def fixed(shape):
    return pl.BlockSpec(shape, lambda g: (0,) * len(shape))


def framed(shape, block, count, reverse, base=0):
    return pl.BlockSpec((block,) + shape[1:], lambda g: (base + (count - 1 - g if reverse else g), 0, 0, 0))


def part_of(bit, value):
    half = value.shape[0] // 2
    return lax.dynamic_slice_in_dim(value, bit[0] * half, half)


def merge(bit, mine, other):
    return jnp.where(bit[0] == 0, jnp.concatenate([mine, other]), jnp.concatenate([other, mine]))


def swap(value, count, distance):
    return lax.ppermute(value, "tm", [(source, source ^ distance) for source in range(count)])


def bits_of(me, levels):
    return [jnp.bitwise_and(lax.shift_right_logical(me, level), 1).reshape(1) for level in range(levels)]


def after(value, *others):
    return lax.optimization_barrier((value, *others))[0]


class Sum:
    def __init__(self, keep, send, main, bits, orders, count):
        self.keep, self.send, self.main, self.count = keep, send, main, count
        self.orders = orders
        self.bits = [jnp.where(bits[0] == 0, bits[even], bits[odd]) for even, odd in zip(*orders)]
        self.stage = 0
        self.left = 2 * len(self.bits)

    def swap(self, value):
        levels = [order[self.stage] for order in self.orders]
        return lax.ppermute(value, "tm", [(source, source ^ (1 << levels[source & 1])) for source in range(self.count)])

    def start(self):
        self.recv = self.swap(self.send)

    def wait(self, *others):
        self.recv = after(self.recv, *others)

    def fold(self):
        total_main = self.keep[: self.main] + self.recv[: self.main]
        total_extra = self.keep[self.main :] + self.recv[self.main :]
        self.stage += 1
        if self.stage == len(self.bits):
            self.send, self.extra = total_main, total_extra
            return
        bit = self.bits[self.stage]
        self.keep = jnp.concatenate([part_of(bit, total_main), total_extra])
        self.send = jnp.concatenate([part_of(1 - bit, total_main), total_extra])
        self.main = self.main // 2

    def step(self):
        if self.left == 0:
            return
        if self.left > len(self.bits):
            self.fold()
        else:
            self.send = merge(self.bits[self.stage], self.send, self.recv)
        self.left -= 1
        if self.left > len(self.bits):
            self.start()
        elif self.left:
            self.stage -= 1
            self.start()


class Carry:
    def __init__(self, message, bits, count, reverse):
        self.message, self.bits, self.count, self.reverse = message, bits, count, reverse
        self.rows = message.shape[0] - 8
        self.reached = jnp.zeros((self.rows // 8, 8, message.shape[1]), F32)
        self.passed = jnp.ones((1, 8, message.shape[1]), F32)
        self.level = 0

    def split(self, message):
        return message[: self.rows].reshape(self.reached.shape), message[self.rows :][None]

    def start(self):
        distance = 1 << self.level
        pairs = [(source, source ^ distance) for source in range(self.count)]
        if self.level == len(self.bits) - 1:
            towards = 0 if self.reverse else distance
            pairs = [pair for pair in pairs if pair[1] & distance == towards]
        self.other = lax.ppermute(self.message, "tm", pairs)

    def combine(self, *others):
        self.other = after(self.other, *others)
        (local, decay), (other_local, other_decay) = self.split(self.message), self.split(self.other)
        later = self.bits[self.level][0] == (0 if self.reverse else 1)
        self.reached = jnp.where(later, self.reached + self.passed * other_local, self.reached)
        self.passed = jnp.where(later, self.passed * other_decay, self.passed)
        local = jnp.where(later, decay * other_local + local, other_decay * local + other_local)
        self.level += 1
        self.message = jnp.concatenate([local.reshape(self.rows, -1), (decay * other_decay)[0]], axis=0)

    def result(self):
        return self.reached.reshape(self.rows, -1)


def body(latents, input_map, output_map, decay_rate, frame_step, cotangent):
    frames, height, breadth, channels = latents.shape
    count = lax.axis_size("tm")
    levels = count.bit_length() - 1
    me = lax.axis_index("tm")
    bits = bits_of(me, levels)
    factor = 1.0 / math.sqrt(frames * count * height * breadth)
    block = 16
    steps = frames // block
    grid = (steps,)
    rate = decay_rate.reshape(1, channels)
    map_rows = height * breadth
    shape = latents.shape
    weights = input_map.shape
    pixels = frames * height * breadth
    flops = 2 * pixels * 6 * channels * channels
    driven_type = pltpu.HBM(shape, F32)
    low_type = pltpu.HBM(shape, BF16)
    map_scratch = pltpu.VMEM((map_rows // 8, 8, channels), F32)
    decay_scratch = pltpu.VMEM((8, channels), F32)
    flip_scratch = pltpu.VMEM(weights, BF16)

    def drive(value, kernel_map, reverse, base, size, start=None):
        specs = [smem(), fixed(rate.shape), framed(shape, block, size, reverse, base), fixed(weights)]
        operands = [frame_step, rate, far(value), far(kernel_map)]
        if start is not None:
            specs.append(fixed((map_rows + 8, channels)))
            operands.append(start)
        return call(
            functools.partial(drive_kernel, reverse, base, start is None),
            (size,),
            specs,
            [framed(shape, block, size, reverse), fixed((map_rows + 8, channels))],
            [pltpu.HBM((size * block,) + shape[1:], F32), jax.ShapeDtypeStruct((map_rows + 8, channels), F32)],
            [map_scratch, decay_scratch, flip_scratch],
            flops * size // steps,
            pixels * channels * 6 * size // steps,
            "pull" if reverse else "drive",
        )(*operands)

    driven, forward_carry = drive(latents, input_map, False, 0, steps)
    forward = Carry(forward_carry, bits, count, False)
    forward.start()
    later = steps // 2
    pulled_late, late_carry = drive(after(cotangent, forward_carry), output_map, True, later, steps - later)
    forward.combine(late_carry)
    forward.start()
    pulled_early, backward_carry = drive(cotangent, output_map, True, 0, later, after(late_carry, forward.message))
    forward.combine(backward_carry)
    forward.start()
    backward = Carry(after(backward_carry, forward.message), bits, count, True)
    backward.start()
    for _ in range(levels - 3):
        forward.combine()
        forward.start()
        backward.combine(forward.message)
        backward.start()
    forward.combine()
    incoming = forward.result()
    backward.combine(incoming)
    backward.start()

    grad_rows = 9 * channels
    half = grad_rows // 2
    sums_scratch = pltpu.VMEM((3, channels, 3 * channels), F32)
    whole_scratch = pltpu.VMEM((grad_rows, channels), F32)
    half_type = jax.ShapeDtypeStruct((half, channels), F32)
    half_extra = jax.ShapeDtypeStruct((half + EXTRA, channels), F32)

    states_low, out_keep, out_send = call(
        functools.partial(state_kernel, factor),
        grid,
        [
            smem(),
            smem(),
            fixed(rate.shape),
            fixed(incoming.shape),
            framed(shape, block, steps, False),
            framed(shape, block, steps, False),
        ],
        [framed(shape, block, steps, False), fixed(half_type.shape), fixed(half_type.shape)],
        [low_type, half_type, half_type],
        [map_scratch, sums_scratch, whole_scratch],
        flops,
        pixels * channels * 8,
        "states",
    )(frame_step, bits[0], rate, after(incoming, backward.message), far(driven), far(cotangent))

    def conv(value, kernel_map, reverse):
        return call(
            functools.partial(conv_kernel, reverse),
            grid,
            [framed(shape, block, steps, False), fixed(weights)],
            framed(shape, block, steps, False),
            low_type,
            [flip_scratch],
            flops,
            pixels * channels * 4,
            "conv",
        )(far(value), far(kernel_map))

    orders = (list(range(levels)), [0] + list(range(2, levels)) + [1])
    backward.combine(out_send)
    backward.start()
    out_sum = Sum(out_keep, after(out_send, backward.message), half, bits, orders, count)
    out_sum.start()
    out_sum.step()
    backward.combine(out_sum.send)
    arriving = backward.result()

    adjoint_low, in_keep, in_send = call(
        functools.partial(adjoint_kernel, factor, steps - later),
        grid,
        [
            smem(),
            smem(),
            fixed(rate.shape),
            fixed(incoming.shape),
            fixed(incoming.shape),
            pl.BlockSpec((block,) + shape[1:], lambda g: (jnp.maximum(steps - 1 - g - later, 0), 0, 0, 0)),
            pl.BlockSpec((block,) + shape[1:], lambda g: (jnp.minimum(steps - 1 - g, later - 1), 0, 0, 0)),
            framed(shape, block, steps, True),
            framed(shape, block, steps, True),
            pl.BlockSpec((1,) + shape[1:], lambda g: (jnp.maximum((steps - 1 - g) * block - 1, 0), 0, 0, 0)),
        ],
        [framed(shape, block, steps, True), fixed(half_extra.shape), fixed(half_extra.shape)],
        [low_type, half_extra, half_extra],
        [map_scratch, decay_scratch, sums_scratch, whole_scratch],
        flops,
        pixels * channels * 10,
        "adjoint",
    )(
        frame_step,
        bits[0],
        rate,
        arriving,
        incoming,
        far(pulled_late),
        far(pulled_early),
        far(latents),
        far(states_low),
        far(states_low),
    )

    out_sum.wait(in_send)
    out_sum.step()
    in_sum = Sum(in_keep, after(in_send, out_sum.send), half, bits, orders, count)
    in_sum.start()
    in_sum.step()
    fillers = [(adjoint_low, input_map, True), (states_low, output_map, False)]
    results = []
    for stage in range(1, 2 * levels):
        if fillers:
            value, kernel_map, reverse = fillers.pop()
            results.append(conv(after(value, in_sum.send), kernel_map, reverse))
            out_sum.wait(results[-1])
        out_sum.wait(in_sum.send)
        out_sum.step()
        in_sum.wait(out_sum.send)
        in_sum.step()
    layer_out, grad_latents = results
    grad_output_map, grad_input_map, rate_rows = out_sum.send, in_sum.send, in_sum.extra
    grad_log_rate = -factor * decay_rate * jnp.sum(rate_rows, axis=0)
    return (
        layer_out,
        grad_latents,
        grad_input_map.reshape(weights),
        grad_output_map.reshape(weights),
        grad_log_rate,
    )


def solution(mesh):
    in_specs = (
        P(("groups", "tm"), None, None, None),
        P(),
        P(),
        P(),
        P(("groups", "tm")),
        P(("groups", "tm"), None, None, None),
    )
    out_specs = (
        P(("groups", "tm"), None, None, None),
        P(("groups", "tm"), None, None, None),
        P("groups", None, None),
        P("groups", None, None),
        P("groups"),
    )
    return jax.shard_map(body, mesh=mesh, in_specs=in_specs, out_specs=out_specs, check_vma=False)
```

```python
import functools
import math

import jax
import jax.numpy as jnp
from jax import lax
from jax.experimental import pallas as pl
from jax.experimental.pallas import tpu as pltpu
from jax.sharding import PartitionSpec as P

F32 = jnp.float32
BF16 = jnp.bfloat16
VMEM_LIMIT = 20 * 1024 * 1024


def column_shifts(value):
    frames, height, breadth, channels = value.shape
    rows = frames * height * breadth
    flat = value.reshape(rows, channels).astype(F32)
    column = lax.broadcasted_iota(jnp.int32, (rows, channels), 0) % breadth
    before = jnp.where(column == 0, 0.0, pltpu.roll(flat, 1, 0)).astype(BF16)
    after = jnp.where(column == breadth - 1, 0.0, pltpu.roll(flat, rows - 1, 0)).astype(BF16)
    return before.reshape(value.shape), value, after.reshape(value.shape)


def conv_rows(value, weights):
    frames, _, breadth, channels = value.shape
    shifted = column_shifts(value)
    pieces = [piece[:, row].reshape(frames * breadth, channels) for row in (0, 1) for piece in shifted]
    patches = jnp.concatenate(pieces, axis=1)
    outs = []
    for first in (3, 0):
        taps = weights[first : first + 6].reshape(6 * channels, weights.shape[2])
        outs.append(jnp.dot(patches, taps, preferred_element_type=F32))
    return outs


def flip_into(flipped_ref, weights_ref):
    for tap in range(9):
        flipped_ref[tap] = weights_ref[8 - tap].T


def decay_of(step, rate):
    return jnp.exp(-(step * rate))


def drive_kernel(reverse, base, fresh, step_ref, rate_ref, value_ref, weights_ref, *refs):
    start_ref, refs = (None, refs) if fresh else (refs[0], refs[1:])
    driven_ref, carry_ref, state, decay, flipped = refs
    index, count = pl.program_id(0), pl.num_programs(0)
    block, _, breadth, channels = driven_ref.shape
    map_rows = state.shape[0] * 8

    @pl.when(index == 0)
    def _():
        state[...] = jnp.zeros_like(state) if fresh else start_ref[:map_rows].reshape(state.shape)
        decay[...] = jnp.ones_like(decay) if fresh else start_ref[map_rows:]
        if reverse:
            flip_into(flipped, weights_ref)

    outs = conv_rows(value_ref[...], flipped if reverse else weights_ref)
    for row, out in enumerate(outs):
        driven_ref[:, row] = out.reshape(block, breadth, channels)
    first = (base + (count - 1 - index if reverse else index)) * block
    rate = jnp.broadcast_to(rate_ref[...], decay.shape)
    total, held = decay[...], state[...]
    for offset in range(block):
        frame = block - 1 - offset if reverse else offset
        factor = decay_of(step_ref[first + frame], rate)
        driven = driven_ref[frame].reshape(state.shape)
        held = factor[None] * (held + driven) if reverse else factor[None] * held + driven
        total = total * factor
    state[...] = held
    decay[...] = total

    @pl.when(index == count - 1)
    def _():
        carry_ref[:map_rows] = held.reshape(map_rows, channels)
        carry_ref[map_rows:] = total


def add_kernel_grad(sums, source, target):
    frames, height, breadth, channels = source.shape
    before, same, after = column_shifts(target)
    taps = jnp.concatenate([after, same, before], axis=-1)

    def contract(left, right):
        return lax.dot_general(
            left.reshape(-1, channels), right.reshape(-1, 3 * channels), (((0,), (0,)), ((), ())), preferred_element_type=F32
        )

    sums[1] += contract(source, taps)
    sums[0] += contract(source[:, 0], taps[:, 1])
    sums[2] += contract(source[:, 1], taps[:, 0])


def split_grad(scale, sums, whole, core, keep_ref, send_ref, rate_sum=None):
    channels = sums.shape[1]
    rows = 9 * channels
    if rate_sum is not None:
        whole[rows:] = jnp.zeros((whole.shape[0] - rows, channels), F32)
        whole[rows : rows + 8] = rate_sum
    for tap in range(9):
        piece = sums[tap // 3, :, (tap % 3) * channels : (tap % 3 + 1) * channels]
        whole[tap * channels : (tap + 1) * channels] = piece * scale
    half = whole.shape[0] // 2
    keep_ref[...] = whole[pl.ds(core * half, half)]
    send_ref[...] = whole[pl.ds((1 - core) * half, half)]


def state_kernel(
    scale, step_ref, core_ref, rate_ref, incoming_ref, driven_ref, cotangent_ref, low_ref, keep_ref, send_ref, state, sums, whole
):
    index, count = pl.program_id(0), pl.num_programs(0)
    block = driven_ref.shape[0]

    @pl.when(index == 0)
    def _():
        state[...] = incoming_ref[...].reshape(state.shape)
        sums[...] = jnp.zeros_like(sums)

    rate = jnp.broadcast_to(rate_ref[...], (8, rate_ref.shape[1]))
    held = state[...]
    for frame in range(block):
        factor = decay_of(step_ref[index * block + frame], rate)
        held = factor[None] * held + driven_ref[frame].reshape(state.shape)
        low_ref[frame] = held.astype(BF16).reshape(low_ref.shape[1:])
    state[...] = held
    add_kernel_grad(sums, low_ref[...], cotangent_ref[...])

    @pl.when(index == count - 1)
    def _():
        split_grad(scale, sums, whole, core_ref[0], keep_ref, send_ref)


def adjoint_kernel(
    scale,
    late_steps,
    step_ref,
    core_ref,
    rate_ref,
    arriving_ref,
    incoming_ref,
    late_ref,
    early_ref,
    latents_ref,
    states_ref,
    previous_ref,
    low_ref,
    keep_ref,
    send_ref,
    carry,
    rate_sum,
    sums,
    whole,
):
    index, count = pl.program_id(0), pl.num_programs(0)
    block = late_ref.shape[0]
    first = (count - 1 - index) * block

    @pl.when(index == 0)
    def _():
        carry[...] = arriving_ref[...].reshape(carry.shape)
        rate_sum[...] = jnp.zeros_like(rate_sum)
        sums[...] = jnp.zeros_like(sums)

    rate = jnp.broadcast_to(rate_ref[...], rate_sum.shape)
    held, summed = carry[...], rate_sum[...]
    for frame in range(block - 1, -1, -1):
        step = step_ref[first + frame]
        pulled = jnp.where(index < late_steps, late_ref[frame], early_ref[frame])
        adjoint = held + pulled.reshape(carry.shape)
        low_ref[frame] = adjoint.astype(BF16).reshape(low_ref.shape[1:])
        held = decay_of(step, rate)[None] * adjoint
        if frame:
            before = states_ref[frame - 1].astype(F32).reshape(carry.shape)
        else:
            before = jnp.where(
                index == count - 1,
                incoming_ref[...].reshape(carry.shape),
                previous_ref[0].astype(F32).reshape(carry.shape),
            )
        summed = summed + step * jnp.sum(held * before, axis=0)
    carry[...] = held
    rate_sum[...] = summed
    add_kernel_grad(sums, latents_ref[...], low_ref[...])

    @pl.when(index == count - 1)
    def _():
        split_grad(scale, sums, whole, core_ref[0], keep_ref, send_ref, summed)


def conv_kernel(reverse, value_ref, weights_ref, *refs):
    out_ref, flipped = refs[-2:]
    if reverse:

        @pl.when(pl.program_id(0) == 0)
        def _():
            flip_into(flipped, weights_ref)

    block, _, breadth, channels = out_ref.shape
    outs = conv_rows(value_ref[...], flipped if reverse else weights_ref)
    for row, out in enumerate(outs):
        out_ref[:, row] = out.astype(BF16).reshape(block, breadth, channels)


def call(kernel, grid, in_specs, out_specs, out_shape, scratch, flops, moved, name, aliases=None):
    return pl.pallas_call(
        kernel,
        grid=grid,
        in_specs=in_specs,
        out_specs=out_specs,
        out_shape=out_shape,
        scratch_shapes=scratch,
        input_output_aliases=aliases or {},
        compiler_params=pltpu.CompilerParams(vmem_limit_bytes=VMEM_LIMIT, dimension_semantics=("arbitrary",) * len(grid)),
        cost_estimate=pl.CostEstimate(flops=flops, bytes_accessed=moved, transcendentals=0),
        name=name,
    )


def far(value):
    return pltpu.with_memory_space_constraint(value, pltpu.HBM)


def smem():
    return pl.BlockSpec(memory_space=pltpu.SMEM)


def fixed(shape):
    return pl.BlockSpec(shape, lambda g: (0,) * len(shape))


def framed(shape, block, count, reverse, base=0):
    return pl.BlockSpec((block,) + shape[1:], lambda g: (base + (count - 1 - g if reverse else g), 0, 0, 0))


def part_of(bit, value):
    half = value.shape[0] // 2
    return lax.dynamic_slice_in_dim(value, bit[0] * half, half)


def merge(bit, mine, other):
    return jnp.where(bit[0] == 0, jnp.concatenate([mine, other]), jnp.concatenate([other, mine]))


def swap(value, count, distance):
    return lax.ppermute(value, "tm", [(source, source ^ distance) for source in range(count)])


def bits_of(me, levels):
    return [jnp.bitwise_and(lax.shift_right_logical(me, level), 1).reshape(1) for level in range(levels)]


def after(value, *others):
    return lax.optimization_barrier((value, *others))[0]


class Sum:
    def __init__(self, keep, send, bits, orders, count):
        self.keep, self.send, self.count = keep, send, count
        self.orders = orders
        self.bits = [jnp.where(bits[0] == 0, bits[even], bits[odd]) for even, odd in zip(*orders)]
        self.stage = 0
        self.left = 2 * len(self.bits)

    def swap(self, value):
        levels = [order[self.stage] for order in self.orders]
        return lax.ppermute(value, "tm", [(source, source ^ (1 << levels[source & 1])) for source in range(self.count)])

    def start(self):
        self.recv = self.swap(self.send)

    def wait(self, *others):
        self.recv = after(self.recv, *others)

    def fold(self):
        total = self.keep + self.recv
        self.stage += 1
        if self.stage == len(self.bits):
            self.send = total
            return
        bit = self.bits[self.stage]
        self.keep, self.send = part_of(bit, total), part_of(1 - bit, total)

    def step(self):
        if self.left == 0:
            return
        if self.left > len(self.bits):
            self.fold()
        else:
            self.send = merge(self.bits[self.stage], self.send, self.recv)
        self.left -= 1
        if self.left > len(self.bits):
            self.start()
        elif self.left:
            self.stage -= 1
            self.start()


class Carry:
    def __init__(self, message, bits, count, reverse):
        self.message, self.bits, self.count, self.reverse = message, bits, count, reverse
        self.rows = message.shape[0] - 8
        self.reached = jnp.zeros((self.rows // 8, 8, message.shape[1]), F32)
        self.passed = jnp.ones((1, 8, message.shape[1]), F32)
        self.level = 0

    def split(self, message):
        return message[: self.rows].reshape(self.reached.shape), message[self.rows :][None]

    def start(self):
        distance = 1 << self.level
        pairs = [(source, source ^ distance) for source in range(self.count)]
        if self.level == len(self.bits) - 1:
            towards = 0 if self.reverse else distance
            pairs = [pair for pair in pairs if pair[1] & distance == towards]
        self.other = lax.ppermute(self.message, "tm", pairs)

    def combine(self, *others):
        self.other = after(self.other, *others)
        (local, decay), (other_local, other_decay) = self.split(self.message), self.split(self.other)
        later = self.bits[self.level][0] == (0 if self.reverse else 1)
        self.reached = jnp.where(later, self.reached + self.passed * other_local, self.reached)
        self.passed = jnp.where(later, self.passed * other_decay, self.passed)
        local = jnp.where(later, decay * other_local + local, other_decay * local + other_local)
        self.level += 1
        self.message = jnp.concatenate([local.reshape(self.rows, -1), (decay * other_decay)[0]], axis=0)

    def start_rest(self):
        runs = self.count // 4
        hops = [-4 * hop if self.reverse else 4 * hop for hop in range(1, runs)]
        self.rest = [
            lax.ppermute(
                self.message, "tm", [(source, source + hop) for source in range(self.count) if 0 <= source + hop < self.count]
            )
            for hop in hops
        ]

    def combine_rest(self, *others):
        held = jnp.zeros_like(self.reached)
        for message in self.rest[::-1]:
            local, decay = self.split(after(message, *others))
            held = local + decay * held
        self.reached = self.reached + self.passed * held

    def result(self):
        return self.reached.reshape(self.rows, -1)


def turns(levels):
    return "icoic" + "oi" * (2 * levels - 3) + "i"


def body(latents, input_map, output_map, decay_rate, frame_step, cotangent):
    frames, height, breadth, channels = latents.shape
    count = lax.axis_size("tm")
    levels = count.bit_length() - 1
    me = lax.axis_index("tm")
    bits = bits_of(me, levels)
    factor = 1.0 / math.sqrt(frames * count * height * breadth)
    block = 16
    steps = frames // block
    grid = (steps,)
    rate = decay_rate.reshape(1, channels)
    map_rows = height * breadth
    shape = latents.shape
    weights = input_map.shape
    pixels = frames * height * breadth
    flops = 2 * pixels * 6 * channels * channels
    driven_type = pltpu.HBM(shape, F32)
    low_type = pltpu.HBM(shape, BF16)
    map_scratch = pltpu.VMEM((map_rows // 8, 8, channels), F32)
    decay_scratch = pltpu.VMEM((8, channels), F32)
    flip_scratch = pltpu.VMEM(weights, BF16)

    def drive(value, kernel_map, reverse, base, size, start=None):
        specs = [smem(), fixed(rate.shape), framed(shape, block, size, reverse, base), fixed(weights)]
        operands = [frame_step, rate, far(value), kernel_map if reverse else far(kernel_map)]
        if start is not None:
            specs.append(fixed((map_rows + 8, channels)))
            operands.append(start)
        return call(
            functools.partial(drive_kernel, reverse, base, start is None),
            (size,),
            specs,
            [framed(shape, block, size, reverse), fixed((map_rows + 8, channels))],
            [pltpu.HBM((size * block,) + shape[1:], F32), jax.ShapeDtypeStruct((map_rows + 8, channels), F32)],
            [map_scratch, decay_scratch, flip_scratch],
            flops * size // steps,
            pixels * channels * 6 * size // steps,
            "pull" if reverse else "drive",
        )(*operands)

    driven, forward_carry = drive(latents, input_map, False, 0, steps)
    forward = Carry(forward_carry, bits, count, False)
    forward.start()
    later = steps // 2
    pulled_late, late_carry = drive(after(cotangent, forward_carry), output_map, True, later, steps - later)
    forward.combine(late_carry)
    forward.start()
    pulled_early, backward_carry = drive(cotangent, output_map, True, 0, later, after(late_carry, forward.message))
    forward.combine(backward_carry)
    forward.start()
    backward = Carry(after(backward_carry, forward.message), bits, count, True)
    backward.start()
    for _ in range(levels - 3):
        forward.combine()
        forward.start()
        if backward.level == 0:
            backward.combine(forward.message)
            backward.start()
    forward.combine()
    incoming = forward.result()
    backward.combine(incoming)
    backward.start_rest()

    grad_rows = 9 * channels
    half = grad_rows // 2
    sums_scratch = pltpu.VMEM((3, channels, 3 * channels), F32)
    whole_scratch = pltpu.VMEM((grad_rows, channels), F32)
    half_type = jax.ShapeDtypeStruct((half, channels), F32)
    padded_rows = grad_rows + 8 * count
    padded_type = jax.ShapeDtypeStruct((padded_rows // 2, channels), F32)

    states_low, out_keep, out_send = call(
        functools.partial(state_kernel, factor),
        grid,
        [
            smem(),
            smem(),
            fixed(rate.shape),
            fixed(incoming.shape),
            framed(shape, block, steps, False),
            framed(shape, block, steps, False),
        ],
        [framed(shape, block, steps, False), fixed(half_type.shape), fixed(half_type.shape)],
        [low_type, half_type, half_type],
        [map_scratch, sums_scratch, whole_scratch],
        flops,
        pixels * channels * 8,
        "states",
    )(frame_step, bits[0], rate, after(incoming, backward.message), far(driven), far(cotangent))

    def conv(value, kernel_map, reverse, base, size, previous=None):
        specs = [framed(shape, block, size, False, base), fixed(weights)]
        operands = [far(value), kernel_map]
        aliases = {}
        if previous is not None:
            specs.append(pl.BlockSpec(memory_space=pl.ANY))
            operands.append(previous)
            aliases = {2: 0}
        return call(
            functools.partial(conv_kernel, reverse),
            (size,),
            specs,
            framed(shape, block, size, False, base),
            low_type,
            [flip_scratch],
            flops * size // steps,
            pixels * channels * 4 * size // steps,
            "conv",
            aliases,
        )(*operands)

    orders = (list(range(levels)), [0] + list(range(2, levels)) + [1])
    backward.combine_rest(out_send)
    arriving = backward.result()
    out_sum = Sum(out_keep, out_send, bits, orders, count)
    out_sum.start()
    out_sum.step()

    adjoint_low, in_keep, in_send = call(
        functools.partial(adjoint_kernel, factor, steps - later),
        grid,
        [
            smem(),
            smem(),
            fixed(rate.shape),
            fixed(incoming.shape),
            fixed(incoming.shape),
            pl.BlockSpec((block,) + shape[1:], lambda g: (jnp.maximum(steps - 1 - g - later, 0), 0, 0, 0)),
            pl.BlockSpec((block,) + shape[1:], lambda g: (jnp.minimum(steps - 1 - g, later - 1), 0, 0, 0)),
            framed(shape, block, steps, True),
            framed(shape, block, steps, True),
            pl.BlockSpec((1,) + shape[1:], lambda g: (jnp.maximum((steps - 1 - g) * block - 1, 0), 0, 0, 0)),
        ],
        [framed(shape, block, steps, True), fixed(padded_type.shape), fixed(padded_type.shape)],
        [low_type, padded_type, padded_type],
        [map_scratch, decay_scratch, sums_scratch, pltpu.VMEM((padded_rows, channels), F32)],
        flops,
        pixels * channels * 10,
        "adjoint",
    )(
        frame_step,
        bits[0],
        rate,
        after(arriving, out_sum.send),
        incoming,
        far(pulled_late),
        far(pulled_early),
        far(latents),
        far(states_low),
        far(states_low),
    )

    out_sum.wait(in_send)
    out_sum.step()
    in_sum = Sum(in_keep, after(in_send, out_sum.send), bits, orders, count)
    in_sum.start()
    covers = [(adjoint_low, input_map, True), (states_low, output_map, False)]
    convs = []
    latest = out_sum.send
    for turn in turns(levels):
        if turn == "c":
            value, kernel_map, reverse = covers.pop()
            convs.append(conv(after(value, latest), kernel_map, reverse, 0, steps))
            latest = convs[-1]
        else:
            one = out_sum if turn == "o" else in_sum
            one.wait(latest)
            one.step()
            latest = one.send
    layer_out, grad_latents = convs
    grad_output_map, grad_input_map = out_sum.send, in_sum.send[:grad_rows]
    rate_rows = in_sum.send[grad_rows : grad_rows + 8]
    grad_log_rate = -factor * decay_rate * jnp.sum(rate_rows, axis=0)
    return (
        layer_out,
        grad_latents,
        grad_input_map.reshape(weights),
        grad_output_map.reshape(weights),
        grad_log_rate,
    )


def solution(mesh):
    in_specs = (
        P(("groups", "tm"), None, None, None),
        P(),
        P(),
        P(),
        P(("groups", "tm")),
        P(("groups", "tm"), None, None, None),
    )
    out_specs = (
        P(("groups", "tm"), None, None, None),
        P(("groups", "tm"), None, None, None),
        P("groups", None, None),
        P("groups", None, None),
        P("groups"),
    )
    return jax.shard_map(body, mesh=mesh, in_specs=in_specs, out_specs=out_specs, check_vma=False)
```

```python
import functools
import math

import jax
import jax.numpy as jnp
from jax import lax
from jax.experimental import pallas as pl
from jax.experimental.pallas import tpu as pltpu
from jax.sharding import PartitionSpec as P

F32 = jnp.float32
BF16 = jnp.bfloat16
VMEM_LIMIT = 20 * 1024 * 1024


def column_shifts(value):
    frames, height, breadth, channels = value.shape
    rows = frames * height * breadth
    flat = value.reshape(rows, channels).astype(F32)
    column = lax.broadcasted_iota(jnp.int32, (rows, channels), 0) % breadth
    before = jnp.where(column == 0, 0.0, pltpu.roll(flat, 1, 0)).astype(BF16)
    after = jnp.where(column == breadth - 1, 0.0, pltpu.roll(flat, rows - 1, 0)).astype(BF16)
    return before.reshape(value.shape), value, after.reshape(value.shape)


def conv_rows(value, weights):
    frames, _, breadth, channels = value.shape
    shifted = column_shifts(value)
    pieces = [piece[:, row].reshape(frames * breadth, channels) for row in (0, 1) for piece in shifted]
    patches = jnp.concatenate(pieces, axis=1)
    outs = []
    for first in (3, 0):
        taps = weights[first : first + 6].reshape(6 * channels, weights.shape[2])
        outs.append(jnp.dot(patches, taps, preferred_element_type=F32))
    return outs


def flip_into(flipped_ref, weights_ref):
    for tap in range(9):
        flipped_ref[tap] = weights_ref[8 - tap].T


def decay_of(step, rate):
    return jnp.exp(-(step * rate))


def drive_kernel(reverse, base, fresh, step_ref, rate_ref, value_ref, weights_ref, *refs):
    start_ref, refs = (None, refs) if fresh else (refs[0], refs[1:])
    driven_ref, carry_ref, state, decay, flipped = refs
    index, count = pl.program_id(0), pl.num_programs(0)
    block, _, breadth, channels = driven_ref.shape
    map_rows = state.shape[0] * 8

    @pl.when(index == 0)
    def _():
        state[...] = jnp.zeros_like(state) if fresh else start_ref[:map_rows].reshape(state.shape)
        decay[...] = jnp.ones_like(decay) if fresh else start_ref[map_rows:]
        if reverse:
            flip_into(flipped, weights_ref)

    outs = conv_rows(value_ref[...], flipped if reverse else weights_ref)
    for row, out in enumerate(outs):
        driven_ref[:, row] = out.reshape(block, breadth, channels)
    first = (base + (count - 1 - index if reverse else index)) * block
    rate = jnp.broadcast_to(rate_ref[...], decay.shape)
    total, held = decay[...], state[...]
    for offset in range(block):
        frame = block - 1 - offset if reverse else offset
        factor = decay_of(step_ref[first + frame], rate)
        driven = driven_ref[frame].reshape(state.shape)
        held = factor[None] * (held + driven) if reverse else factor[None] * held + driven
        total = total * factor
    state[...] = held
    decay[...] = total

    @pl.when(index == count - 1)
    def _():
        carry_ref[:map_rows] = held.reshape(map_rows, channels)
        carry_ref[map_rows:] = total


def add_kernel_grad(sums, source, target):
    frames, height, breadth, channels = source.shape
    before, same, after = column_shifts(target)
    taps = jnp.concatenate([after, same, before], axis=-1)

    def contract(left, right):
        return lax.dot_general(
            left.reshape(-1, channels), right.reshape(-1, 3 * channels), (((0,), (0,)), ((), ())), preferred_element_type=F32
        )

    sums[1] += contract(source, taps)
    sums[0] += contract(source[:, 0], taps[:, 1])
    sums[2] += contract(source[:, 1], taps[:, 0])


def split_grad(scale, sums, whole, core, keep_ref, send_ref, rate_sum=None):
    channels = sums.shape[1]
    rows = 9 * channels
    if rate_sum is not None:
        whole[rows:] = jnp.zeros((whole.shape[0] - rows, channels), F32)
        whole[rows : rows + 8] = rate_sum
    for tap in range(9):
        piece = sums[tap // 3, :, (tap % 3) * channels : (tap % 3 + 1) * channels]
        whole[tap * channels : (tap + 1) * channels] = piece * scale
    half = whole.shape[0] // 2
    keep_ref[...] = whole[pl.ds(core * half, half)]
    send_ref[...] = whole[pl.ds((1 - core) * half, half)]


def state_kernel(
    scale, step_ref, core_ref, rate_ref, incoming_ref, driven_ref, cotangent_ref, low_ref, keep_ref, send_ref, state, sums, whole
):
    index, count = pl.program_id(0), pl.num_programs(0)
    block = driven_ref.shape[0]

    @pl.when(index == 0)
    def _():
        state[...] = incoming_ref[...].reshape(state.shape)
        sums[...] = jnp.zeros_like(sums)

    rate = jnp.broadcast_to(rate_ref[...], (8, rate_ref.shape[1]))
    held = state[...]
    for frame in range(block):
        factor = decay_of(step_ref[index * block + frame], rate)
        held = factor[None] * held + driven_ref[frame].reshape(state.shape)
        low_ref[frame] = held.astype(BF16).reshape(low_ref.shape[1:])
    state[...] = held
    add_kernel_grad(sums, low_ref[...], cotangent_ref[...])

    @pl.when(index == count - 1)
    def _():
        split_grad(scale, sums, whole, core_ref[0], keep_ref, send_ref)


def adjoint_kernel(
    scale,
    late_steps,
    step_ref,
    core_ref,
    rate_ref,
    arriving_ref,
    incoming_ref,
    late_ref,
    early_ref,
    latents_ref,
    states_ref,
    previous_ref,
    low_ref,
    keep_ref,
    send_ref,
    carry,
    rate_sum,
    sums,
    whole,
):
    index, count = pl.program_id(0), pl.num_programs(0)
    block = late_ref.shape[0]
    first = (count - 1 - index) * block

    @pl.when(index == 0)
    def _():
        carry[...] = arriving_ref[...].reshape(carry.shape)
        rate_sum[...] = jnp.zeros_like(rate_sum)
        sums[...] = jnp.zeros_like(sums)

    rate = jnp.broadcast_to(rate_ref[...], rate_sum.shape)
    held, summed = carry[...], rate_sum[...]
    for frame in range(block - 1, -1, -1):
        step = step_ref[first + frame]
        pulled = jnp.where(index < late_steps, late_ref[frame], early_ref[frame])
        adjoint = held + pulled.reshape(carry.shape)
        low_ref[frame] = adjoint.astype(BF16).reshape(low_ref.shape[1:])
        held = decay_of(step, rate)[None] * adjoint
        if frame:
            before = states_ref[frame - 1].astype(F32).reshape(carry.shape)
        else:
            before = jnp.where(
                index == count - 1,
                incoming_ref[...].reshape(carry.shape),
                previous_ref[0].astype(F32).reshape(carry.shape),
            )
        summed = summed + step * jnp.sum(held * before, axis=0)
    carry[...] = held
    rate_sum[...] = summed
    add_kernel_grad(sums, latents_ref[...], low_ref[...])

    @pl.when(index == count - 1)
    def _():
        split_grad(scale, sums, whole, core_ref[0], keep_ref, send_ref, summed)


def conv_kernel(reverse, value_ref, weights_ref, *refs):
    out_ref, flipped = refs[-2:]
    if reverse:

        @pl.when(pl.program_id(0) == 0)
        def _():
            flip_into(flipped, weights_ref)

    block, _, breadth, channels = out_ref.shape
    outs = conv_rows(value_ref[...], flipped if reverse else weights_ref)
    for row, out in enumerate(outs):
        out_ref[:, row] = out.astype(BF16).reshape(block, breadth, channels)


def call(kernel, grid, in_specs, out_specs, out_shape, scratch, flops, moved, name, aliases=None):
    return pl.pallas_call(
        kernel,
        grid=grid,
        in_specs=in_specs,
        out_specs=out_specs,
        out_shape=out_shape,
        scratch_shapes=scratch,
        input_output_aliases=aliases or {},
        compiler_params=pltpu.CompilerParams(vmem_limit_bytes=VMEM_LIMIT, dimension_semantics=("arbitrary",) * len(grid)),
        cost_estimate=pl.CostEstimate(flops=flops, bytes_accessed=moved, transcendentals=0),
        name=name,
    )


def far(value):
    return pltpu.with_memory_space_constraint(value, pltpu.HBM)


def smem():
    return pl.BlockSpec(memory_space=pltpu.SMEM)


def fixed(shape):
    return pl.BlockSpec(shape, lambda g: (0,) * len(shape))


def framed(shape, block, count, reverse, base=0):
    return pl.BlockSpec((block,) + shape[1:], lambda g: (base + (count - 1 - g if reverse else g), 0, 0, 0))


def part_of(bit, value):
    half = value.shape[0] // 2
    return lax.dynamic_slice_in_dim(value, bit[0] * half, half)


def merge(bit, mine, other, rows=None):
    if rows is None or rows == 2 * mine.shape[0]:
        return jnp.where(bit[0] == 0, jnp.concatenate([mine, other]), jnp.concatenate([other, mine]))
    cut = rows - mine.shape[0]
    first, last = (mine, other[: cut + 8]), (other, mine[: cut + 8])
    main = jnp.where(bit[0] == 0, jnp.concatenate([first[0], first[1][:cut]]), jnp.concatenate([last[0], last[1][:cut]]))
    return main, jnp.where(bit[0] == 0, first[1][cut:], last[1][cut:])


def swap(value, count, distance):
    return lax.ppermute(value, "tm", [(source, source ^ distance) for source in range(count)])


def bits_of(me, levels):
    return [jnp.bitwise_and(lax.shift_right_logical(me, level), 1).reshape(1) for level in range(levels)]


def after(value, *others):
    return lax.optimization_barrier((value, *others))[0]


class Sum:
    def __init__(self, keep, send, bits, orders, count, rows):
        self.keep, self.send, self.count, self.rows = keep, send, count, rows
        self.orders = orders
        self.bits = [jnp.where(bits[0] == 0, bits[even], bits[odd]) for even, odd in zip(*orders)]
        self.stage = 0
        self.left = 2 * len(self.bits)

    def swap(self, value):
        levels = [order[self.stage] for order in self.orders]
        return lax.ppermute(value, "tm", [(source, source ^ (1 << levels[source & 1])) for source in range(self.count)])

    def start(self):
        self.recv = self.swap(self.send)

    def wait(self, *others):
        self.recv = after(self.recv, *others)

    def fold(self):
        total = self.keep + self.recv
        self.stage += 1
        if self.stage == len(self.bits):
            self.send = total
            return
        bit = self.bits[self.stage]
        self.keep, self.send = part_of(bit, total), part_of(1 - bit, total)

    def step(self):
        if self.left == 0:
            return
        if self.left > len(self.bits):
            self.fold()
        else:
            self.send = merge(self.bits[self.stage], self.send, self.recv, self.rows if self.left == 1 else None)
        self.left -= 1
        if self.left > len(self.bits):
            self.start()
        elif self.left:
            self.stage -= 1
            self.start()


class Carry:
    def __init__(self, message, bits, count, reverse):
        self.message, self.bits, self.count, self.reverse = message, bits, count, reverse
        self.rows = message.shape[0] - 8
        self.reached = jnp.zeros((self.rows // 8, 8, message.shape[1]), F32)
        self.passed = jnp.ones((1, 8, message.shape[1]), F32)
        self.level = 0

    def split(self, message):
        return message[: self.rows].reshape(self.reached.shape), message[self.rows :][None]

    def start(self):
        distance = 1 << self.level
        pairs = [(source, source ^ distance) for source in range(self.count)]
        if self.level == len(self.bits) - 1:
            towards = 0 if self.reverse else distance
            pairs = [pair for pair in pairs if pair[1] & distance == towards]
        self.other = lax.ppermute(self.message, "tm", pairs)

    def combine(self, *others):
        self.other = after(self.other, *others)
        (local, decay), (other_local, other_decay) = self.split(self.message), self.split(self.other)
        later = self.bits[self.level][0] == (0 if self.reverse else 1)
        self.reached = jnp.where(later, self.reached + self.passed * other_local, self.reached)
        self.passed = jnp.where(later, self.passed * other_decay, self.passed)
        local = jnp.where(later, decay * other_local + local, other_decay * local + other_local)
        self.level += 1
        self.message = jnp.concatenate([local.reshape(self.rows, -1), (decay * other_decay)[0]], axis=0)

    def start_rest(self):
        runs = self.count // 4
        hops = [-4 * hop if self.reverse else 4 * hop for hop in range(1, runs)]
        self.rest = [
            lax.ppermute(
                self.message, "tm", [(source, source + hop) for source in range(self.count) if 0 <= source + hop < self.count]
            )
            for hop in hops
        ]

    def combine_rest(self, *others):
        held = jnp.zeros_like(self.reached)
        for message in self.rest[::-1]:
            local, decay = self.split(after(message, *others))
            held = local + decay * held
        self.reached = self.reached + self.passed * held

    def result(self):
        return self.reached.reshape(self.rows, -1)


def turns(levels):
    return "icoioic" + "oi" * (2 * levels - 4) + "i"


def body(latents, input_map, output_map, decay_rate, frame_step, cotangent):
    frames, height, breadth, channels = latents.shape
    count = lax.axis_size("tm")
    levels = count.bit_length() - 1
    me = lax.axis_index("tm")
    bits = bits_of(me, levels)
    factor = 1.0 / math.sqrt(frames * count * height * breadth)
    block = 16
    steps = frames // block
    grid = (steps,)
    rate = decay_rate.reshape(1, channels)
    map_rows = height * breadth
    shape = latents.shape
    weights = input_map.shape
    pixels = frames * height * breadth
    flops = 2 * pixels * 6 * channels * channels
    driven_type = pltpu.HBM(shape, F32)
    low_type = pltpu.HBM(shape, BF16)
    map_scratch = pltpu.VMEM((map_rows // 8, 8, channels), F32)
    decay_scratch = pltpu.VMEM((8, channels), F32)
    flip_scratch = pltpu.VMEM(weights, BF16)

    def drive(value, kernel_map, reverse, base, size, start=None):
        specs = [smem(), fixed(rate.shape), framed(shape, block, size, reverse, base), fixed(weights)]
        operands = [far(frame_step), far(rate), far(value), kernel_map if reverse else far(kernel_map)]
        if start is not None:
            specs.append(fixed((map_rows + 8, channels)))
            operands.append(start)
        return call(
            functools.partial(drive_kernel, reverse, base, start is None),
            (size,),
            specs,
            [framed(shape, block, size, reverse), fixed((map_rows + 8, channels))],
            [pltpu.HBM((size * block,) + shape[1:], F32), jax.ShapeDtypeStruct((map_rows + 8, channels), F32)],
            [map_scratch, decay_scratch, flip_scratch],
            flops * size // steps,
            pixels * channels * 6 * size // steps,
            "pull" if reverse else "drive",
        )(*operands)

    driven, forward_carry = drive(latents, input_map, False, 0, steps)
    forward = Carry(forward_carry, bits, count, False)
    forward.start()
    later = steps // 2
    pulled_late, late_carry = drive(after(cotangent, forward_carry), output_map, True, later, steps - later)
    forward.combine(late_carry)
    forward.start()
    pulled_early, backward_carry = drive(cotangent, output_map, True, 0, later, after(late_carry, forward.message))
    forward.combine(backward_carry)
    forward.start()
    backward = Carry(after(backward_carry, forward.message), bits, count, True)
    backward.start()
    for _ in range(levels - 3):
        forward.combine()
        forward.start()
        if backward.level == 0:
            backward.combine(forward.message)
            backward.start()
    forward.combine()
    incoming = forward.result()
    backward.combine(incoming)
    backward.start_rest()

    grad_rows = 9 * channels
    half = grad_rows // 2
    sums_scratch = pltpu.VMEM((3, channels, 3 * channels), F32)
    whole_scratch = pltpu.VMEM((grad_rows, channels), F32)
    half_type = jax.ShapeDtypeStruct((half, channels), F32)
    padded_rows = grad_rows + 8 * count
    padded_type = jax.ShapeDtypeStruct((padded_rows // 2, channels), F32)

    states_low, out_keep, out_send = call(
        functools.partial(state_kernel, factor),
        grid,
        [
            smem(),
            smem(),
            fixed(rate.shape),
            fixed(incoming.shape),
            framed(shape, block, steps, False),
            framed(shape, block, steps, False),
        ],
        [framed(shape, block, steps, False), fixed(half_type.shape), fixed(half_type.shape)],
        [low_type, half_type, half_type],
        [map_scratch, sums_scratch, whole_scratch],
        flops,
        pixels * channels * 8,
        "states",
    )(frame_step, bits[0], rate, after(incoming, backward.message), far(driven), far(cotangent))

    def conv(value, kernel_map, reverse, base, size, previous=None):
        specs = [framed(shape, block, size, False, base), fixed(weights)]
        operands = [far(value), kernel_map]
        aliases = {}
        if previous is not None:
            specs.append(pl.BlockSpec(memory_space=pl.ANY))
            operands.append(previous)
            aliases = {2: 0}
        return call(
            functools.partial(conv_kernel, reverse),
            (size,),
            specs,
            framed(shape, block, size, False, base),
            low_type,
            [flip_scratch],
            flops * size // steps,
            pixels * channels * 4 * size // steps,
            "conv",
            aliases,
        )(*operands)

    orders = (list(range(levels)), [0, 2, 1] + list(range(3, levels)))
    backward.combine_rest(out_send)
    arriving = backward.result()
    out_sum = Sum(out_keep, out_send, bits, orders, count, grad_rows)
    out_sum.start()
    out_sum.step()

    adjoint_low, in_keep, in_send = call(
        functools.partial(adjoint_kernel, factor, steps - later),
        grid,
        [
            smem(),
            smem(),
            fixed(rate.shape),
            fixed(incoming.shape),
            fixed(incoming.shape),
            pl.BlockSpec((block,) + shape[1:], lambda g: (jnp.maximum(steps - 1 - g - later, 0), 0, 0, 0)),
            pl.BlockSpec((block,) + shape[1:], lambda g: (jnp.minimum(steps - 1 - g, later - 1), 0, 0, 0)),
            framed(shape, block, steps, True),
            framed(shape, block, steps, True),
            pl.BlockSpec((1,) + shape[1:], lambda g: (jnp.maximum((steps - 1 - g) * block - 1, 0), 0, 0, 0)),
        ],
        [framed(shape, block, steps, True), fixed(padded_type.shape), fixed(padded_type.shape)],
        [low_type, padded_type, padded_type],
        [map_scratch, decay_scratch, sums_scratch, pltpu.VMEM((padded_rows, channels), F32)],
        flops,
        pixels * channels * 10,
        "adjoint",
    )(
        frame_step,
        bits[0],
        rate,
        after(arriving, out_sum.send),
        incoming,
        far(pulled_late),
        far(pulled_early),
        far(latents),
        far(states_low),
        far(states_low),
    )

    out_sum.wait(in_send)
    out_sum.step()
    in_sum = Sum(in_keep, after(in_send, out_sum.send), bits, orders, count, grad_rows)
    in_sum.start()
    covers = [(adjoint_low, input_map, True), (states_low, output_map, False)]
    convs = []
    latest = out_sum.send
    for turn in turns(levels):
        if turn == "c":
            value, kernel_map, reverse = covers.pop()
            convs.append(conv(after(value, latest), kernel_map, reverse, 0, steps))
            latest = convs[-1]
        else:
            one = out_sum if turn == "o" else in_sum
            one.wait(latest)
            one.step()
            latest = one.send
    layer_out, grad_latents = convs
    grad_output_map, (grad_input_map, rate_rows) = out_sum.send, in_sum.send
    grad_log_rate = -factor * decay_rate * jnp.sum(rate_rows, axis=0)
    return (
        layer_out,
        grad_latents,
        grad_input_map.reshape(weights),
        grad_output_map.reshape(weights),
        grad_log_rate,
    )


def solution(mesh):
    in_specs = (
        P(("groups", "tm"), None, None, None),
        P(),
        P(),
        P(),
        P(("groups", "tm")),
        P(("groups", "tm"), None, None, None),
    )
    out_specs = (
        P(("groups", "tm"), None, None, None),
        P(("groups", "tm"), None, None, None),
        P("groups", None, None),
        P("groups", None, None),
        P("groups"),
    )
    return jax.shard_map(body, mesh=mesh, in_specs=in_specs, out_specs=out_specs, check_vma=False)
```

```python
import functools
import math

import jax
import jax.numpy as jnp
from jax import lax
from jax.experimental import pallas as pl
from jax.experimental.pallas import tpu as pltpu
from jax.sharding import PartitionSpec as P

F32 = jnp.float32
BF16 = jnp.bfloat16
VMEM_LIMIT = 36 * 1024 * 1024


def column_shifts(value):
    frames, height, breadth, channels = value.shape
    rows = frames * height * breadth
    flat = value.reshape(rows, channels).astype(F32)
    column = lax.broadcasted_iota(jnp.int32, (rows, channels), 0) % breadth
    before = jnp.where(column == 0, 0.0, pltpu.roll(flat, 1, 0)).astype(BF16)
    after = jnp.where(column == breadth - 1, 0.0, pltpu.roll(flat, rows - 1, 0)).astype(BF16)
    return before.reshape(value.shape), value, after.reshape(value.shape)


def conv_rows(value, weights):
    frames, _, breadth, channels = value.shape
    shifted = column_shifts(value)
    pieces = [piece[:, row].reshape(frames * breadth, channels) for row in (0, 1) for piece in shifted]
    patches = jnp.concatenate(pieces, axis=1)
    outs = []
    for first in (3, 0):
        taps = weights[first : first + 6].reshape(6 * channels, weights.shape[2])
        outs.append(jnp.dot(patches, taps, preferred_element_type=F32))
    return outs


def flip_into(flipped_ref, weights_ref):
    for tap in range(9):
        flipped_ref[tap] = weights_ref[8 - tap].T


def decay_of(step, rate):
    return jnp.exp(-(step * rate))


def drive_kernel(reverse, base, fresh, step_ref, rate_ref, value_ref, weights_ref, *refs):
    start_ref, refs = (None, refs) if fresh else (refs[0], refs[1:])
    driven_ref, carry_ref, state, decay, flipped = refs
    index, count = pl.program_id(0), pl.num_programs(0)
    block, _, breadth, channels = driven_ref.shape
    map_rows = state.shape[0] * 8

    @pl.when(index == 0)
    def _():
        state[...] = jnp.zeros_like(state) if fresh else start_ref[:map_rows].reshape(state.shape)
        decay[...] = jnp.ones_like(decay) if fresh else start_ref[map_rows:]
        if reverse:
            flip_into(flipped, weights_ref)

    outs = conv_rows(value_ref[...], flipped if reverse else weights_ref)
    for row, out in enumerate(outs):
        driven_ref[:, row] = out.reshape(block, breadth, channels)
    first = (base + (count - 1 - index if reverse else index)) * block
    rate = jnp.broadcast_to(rate_ref[...], decay.shape)
    total, held = decay[...], state[...]
    for offset in range(block):
        frame = block - 1 - offset if reverse else offset
        factor = decay_of(step_ref[first + frame], rate)
        driven = driven_ref[frame].reshape(state.shape)
        held = factor[None] * (held + driven) if reverse else factor[None] * held + driven
        total = total * factor
    state[...] = held
    decay[...] = total

    @pl.when(index == count - 1)
    def _():
        carry_ref[:map_rows] = held.reshape(map_rows, channels)
        carry_ref[map_rows:] = total


def add_kernel_grad(sums, source, target):
    frames, height, breadth, channels = source.shape
    before, same, after = column_shifts(target)
    taps = jnp.concatenate([after, same, before], axis=-1)

    def contract(left, right):
        return lax.dot_general(
            left.reshape(-1, channels), right.reshape(-1, 3 * channels), (((0,), (0,)), ((), ())), preferred_element_type=F32
        )

    sums[1] += contract(source, taps)
    sums[0] += contract(source[:, 0], taps[:, 1])
    sums[2] += contract(source[:, 1], taps[:, 0])


def split_grad(scale, sums, whole, core, keep_ref, send_ref, rate_sum=None):
    channels = sums.shape[1]
    rows = 9 * channels
    if rate_sum is not None:
        whole[rows:] = jnp.zeros((whole.shape[0] - rows, channels), F32)
        whole[rows : rows + 8] = rate_sum
    for tap in range(9):
        piece = sums[tap // 3, :, (tap % 3) * channels : (tap % 3 + 1) * channels]
        whole[tap * channels : (tap + 1) * channels] = piece * scale
    half = whole.shape[0] // 2
    keep_ref[...] = whole[pl.ds(core * half, half)]
    send_ref[...] = whole[pl.ds((1 - core) * half, half)]


def state_kernel(
    scale, step_ref, core_ref, rate_ref, incoming_ref, driven_ref, cotangent_ref, low_ref, keep_ref, send_ref, state, sums, whole
):
    index, count = pl.program_id(0), pl.num_programs(0)
    block = driven_ref.shape[0]

    @pl.when(index == 0)
    def _():
        state[...] = incoming_ref[...].reshape(state.shape)
        sums[...] = jnp.zeros_like(sums)

    rate = jnp.broadcast_to(rate_ref[...], (8, rate_ref.shape[1]))
    held = state[...]
    for frame in range(block):
        factor = decay_of(step_ref[index * block + frame], rate)
        held = factor[None] * held + driven_ref[frame].reshape(state.shape)
        low_ref[frame] = held.astype(BF16).reshape(low_ref.shape[1:])
    state[...] = held
    add_kernel_grad(sums, low_ref[...], cotangent_ref[...])

    @pl.when(index == count - 1)
    def _():
        split_grad(scale, sums, whole, core_ref[0], keep_ref, send_ref)


def adjoint_kernel(
    scale,
    late_steps,
    step_ref,
    core_ref,
    rate_ref,
    arriving_ref,
    incoming_ref,
    late_ref,
    early_ref,
    latents_ref,
    states_ref,
    previous_ref,
    low_ref,
    keep_ref,
    send_ref,
    carry,
    rate_sum,
    sums,
    whole,
):
    index, count = pl.program_id(0), pl.num_programs(0)
    block = late_ref.shape[0]
    first = (count - 1 - index) * block

    @pl.when(index == 0)
    def _():
        carry[...] = arriving_ref[...].reshape(carry.shape)
        rate_sum[...] = jnp.zeros_like(rate_sum)
        sums[...] = jnp.zeros_like(sums)

    rate = jnp.broadcast_to(rate_ref[...], rate_sum.shape)
    held, summed = carry[...], rate_sum[...]
    for frame in range(block - 1, -1, -1):
        step = step_ref[first + frame]
        pulled = jnp.where(index < late_steps, late_ref[frame], early_ref[frame])
        adjoint = held + pulled.reshape(carry.shape)
        low_ref[frame] = adjoint.astype(BF16).reshape(low_ref.shape[1:])
        held = decay_of(step, rate)[None] * adjoint
        if frame:
            before = states_ref[frame - 1].astype(F32).reshape(carry.shape)
        else:
            before = jnp.where(
                index == count - 1,
                incoming_ref[...].reshape(carry.shape),
                previous_ref[0].astype(F32).reshape(carry.shape),
            )
        summed = summed + step * jnp.sum(held * before, axis=0)
    carry[...] = held
    rate_sum[...] = summed
    add_kernel_grad(sums, latents_ref[...], low_ref[...])

    @pl.when(index == count - 1)
    def _():
        split_grad(scale, sums, whole, core_ref[0], keep_ref, send_ref, summed)


def conv_kernel(reverse, value_ref, weights_ref, *refs):
    out_ref, flipped = refs[-2:]
    if reverse:

        @pl.when(pl.program_id(0) == 0)
        def _():
            flip_into(flipped, weights_ref)

    block, _, breadth, channels = out_ref.shape
    outs = conv_rows(value_ref[...], flipped if reverse else weights_ref)
    for row, out in enumerate(outs):
        out_ref[:, row] = out.astype(BF16).reshape(block, breadth, channels)


def call(kernel, grid, in_specs, out_specs, out_shape, scratch, flops, moved, name, aliases=None):
    return pl.pallas_call(
        kernel,
        grid=grid,
        in_specs=in_specs,
        out_specs=out_specs,
        out_shape=out_shape,
        scratch_shapes=scratch,
        input_output_aliases=aliases or {},
        compiler_params=pltpu.CompilerParams(vmem_limit_bytes=VMEM_LIMIT, dimension_semantics=("arbitrary",) * len(grid)),
        cost_estimate=pl.CostEstimate(flops=flops, bytes_accessed=moved, transcendentals=0),
        name=name,
    )


def far(value):
    return pltpu.with_memory_space_constraint(value, pltpu.HBM)


def smem():
    return pl.BlockSpec(memory_space=pltpu.SMEM)


def fixed(shape):
    return pl.BlockSpec(shape, lambda g: (0,) * len(shape))


def framed(shape, block, count, reverse, base=0):
    return pl.BlockSpec((block,) + shape[1:], lambda g: (base + (count - 1 - g if reverse else g), 0, 0, 0))


def part_of(bit, value):
    half = value.shape[0] // 2
    return lax.dynamic_slice_in_dim(value, bit[0] * half, half)


def merge(bit, mine, other, rows=None):
    if rows is None or rows == 2 * mine.shape[0]:
        return jnp.where(bit[0] == 0, jnp.concatenate([mine, other]), jnp.concatenate([other, mine]))
    cut = rows - mine.shape[0]
    first, last = (mine, other[: cut + 8]), (other, mine[: cut + 8])
    main = jnp.where(bit[0] == 0, jnp.concatenate([first[0], first[1][:cut]]), jnp.concatenate([last[0], last[1][:cut]]))
    return main, jnp.where(bit[0] == 0, first[1][cut:], last[1][cut:])


def swap(value, count, distance):
    return lax.ppermute(value, "tm", [(source, source ^ distance) for source in range(count)])


def bits_of(me, levels):
    return [jnp.bitwise_and(lax.shift_right_logical(me, level), 1).reshape(1) for level in range(levels)]


def after(value, *others):
    return lax.optimization_barrier((value, *others))[0]


class Sum:
    def __init__(self, keep, send, bits, orders, count, rows):
        self.keep, self.send, self.count, self.rows = keep, send, count, rows
        self.orders = orders
        self.bits = [jnp.where(bits[0] == 0, bits[even], bits[odd]) for even, odd in zip(*orders)]
        self.stage = 0
        self.left = 2 * len(self.bits)

    def swap(self, value):
        levels = [order[self.stage] for order in self.orders]
        return lax.ppermute(value, "tm", [(source, source ^ (1 << levels[source & 1])) for source in range(self.count)])

    def start(self):
        self.recv = self.swap(self.send)

    def wait(self, *others):
        self.recv = after(self.recv, *others)

    def fold(self):
        total = self.keep + self.recv
        self.stage += 1
        if self.stage == len(self.bits):
            self.send = total
            return
        bit = self.bits[self.stage]
        self.keep, self.send = part_of(bit, total), part_of(1 - bit, total)

    def step(self):
        if self.left == 0:
            return
        if self.left > len(self.bits):
            self.fold()
        else:
            self.send = merge(self.bits[self.stage], self.send, self.recv, self.rows if self.left == 1 else None)
        self.left -= 1
        if self.left > len(self.bits):
            self.start()
        elif self.left:
            self.stage -= 1
            self.start()


class Carry:
    def __init__(self, message, bits, count, reverse):
        self.message, self.bits, self.count, self.reverse = message, bits, count, reverse
        self.rows = message.shape[0] - 8
        self.reached = jnp.zeros((self.rows // 8, 8, message.shape[1]), F32)
        self.passed = jnp.ones((1, 8, message.shape[1]), F32)
        self.level = 0

    def split(self, message):
        return message[: self.rows].reshape(self.reached.shape), message[self.rows :][None]

    def start(self):
        distance = 1 << self.level
        pairs = [(source, source ^ distance) for source in range(self.count)]
        if self.level == len(self.bits) - 1:
            towards = 0 if self.reverse else distance
            pairs = [pair for pair in pairs if pair[1] & distance == towards]
        self.other = lax.ppermute(self.message, "tm", pairs)

    def combine(self, *others):
        self.other = after(self.other, *others)
        (local, decay), (other_local, other_decay) = self.split(self.message), self.split(self.other)
        later = self.bits[self.level][0] == (0 if self.reverse else 1)
        self.reached = jnp.where(later, self.reached + self.passed * other_local, self.reached)
        self.passed = jnp.where(later, self.passed * other_decay, self.passed)
        local = jnp.where(later, decay * other_local + local, other_decay * local + other_local)
        self.level += 1
        self.message = jnp.concatenate([local.reshape(self.rows, -1), (decay * other_decay)[0]], axis=0)

    def start_rest(self):
        runs = self.count // 4
        hops = [-4 * hop if self.reverse else 4 * hop for hop in range(1, runs)]
        self.rest = [
            lax.ppermute(
                self.message, "tm", [(source, source + hop) for source in range(self.count) if 0 <= source + hop < self.count]
            )
            for hop in hops
        ]

    def combine_rest(self, *others):
        held = jnp.zeros_like(self.reached)
        for message in self.rest[::-1]:
            local, decay = self.split(after(message, *others))
            held = local + decay * held
        self.reached = self.reached + self.passed * held

    def result(self):
        return self.reached.reshape(self.rows, -1)


def turns(levels):
    return "icoioic" + "oi" * (2 * levels - 4) + "i"


def body(latents, input_map, output_map, decay_rate, frame_step, cotangent):
    frames, height, breadth, channels = latents.shape
    count = lax.axis_size("tm")
    levels = count.bit_length() - 1
    me = lax.axis_index("tm")
    bits = bits_of(me, levels)
    factor = 1.0 / math.sqrt(frames * count * height * breadth)
    block = 32
    steps = frames // block
    grid = (steps,)
    rate = decay_rate.reshape(1, channels)
    map_rows = height * breadth
    shape = latents.shape
    weights = input_map.shape
    pixels = frames * height * breadth
    flops = 2 * pixels * 6 * channels * channels
    driven_type = pltpu.HBM(shape, F32)
    low_type = pltpu.HBM(shape, BF16)
    map_scratch = pltpu.VMEM((map_rows // 8, 8, channels), F32)
    decay_scratch = pltpu.VMEM((8, channels), F32)
    flip_scratch = pltpu.VMEM(weights, BF16)

    def drive(value, kernel_map, reverse, base, size, start=None):
        specs = [smem(), fixed(rate.shape), framed(shape, block, size, reverse, base), fixed(weights)]
        operands = [far(frame_step), far(rate), far(value), kernel_map if reverse else far(kernel_map)]
        if start is not None:
            specs.append(fixed((map_rows + 8, channels)))
            operands.append(start)
        return call(
            functools.partial(drive_kernel, reverse, base, start is None),
            (size,),
            specs,
            [framed(shape, block, size, reverse), fixed((map_rows + 8, channels))],
            [pltpu.HBM((size * block,) + shape[1:], F32), jax.ShapeDtypeStruct((map_rows + 8, channels), F32)],
            [map_scratch, decay_scratch, flip_scratch],
            flops * size // steps,
            pixels * channels * 6 * size // steps,
            "pull" if reverse else "drive",
        )(*operands)

    driven, forward_carry = drive(latents, input_map, False, 0, steps)
    forward = Carry(forward_carry, bits, count, False)
    forward.start()
    later = steps // 2
    pulled_late, late_carry = drive(after(cotangent, forward_carry), output_map, True, later, steps - later)
    forward.combine(late_carry)
    forward.start()
    pulled_early, backward_carry = drive(cotangent, output_map, True, 0, later, after(late_carry, forward.message))
    forward.combine(backward_carry)
    forward.start()
    backward = Carry(after(backward_carry, forward.message), bits, count, True)
    backward.start()
    for _ in range(levels - 3):
        forward.combine()
        forward.start()
        if backward.level == 0:
            backward.combine(forward.message)
            backward.start()
    forward.combine()
    incoming = forward.result()
    backward.combine(incoming)
    backward.start_rest()

    grad_rows = 9 * channels
    half = grad_rows // 2
    sums_scratch = pltpu.VMEM((3, channels, 3 * channels), F32)
    whole_scratch = pltpu.VMEM((grad_rows, channels), F32)
    half_type = jax.ShapeDtypeStruct((half, channels), F32)
    padded_rows = grad_rows + 8 * count
    padded_type = jax.ShapeDtypeStruct((padded_rows // 2, channels), F32)

    states_low, out_keep, out_send = call(
        functools.partial(state_kernel, factor),
        grid,
        [
            smem(),
            smem(),
            fixed(rate.shape),
            fixed(incoming.shape),
            framed(shape, block, steps, False),
            framed(shape, block, steps, False),
        ],
        [framed(shape, block, steps, False), fixed(half_type.shape), fixed(half_type.shape)],
        [low_type, half_type, half_type],
        [map_scratch, sums_scratch, whole_scratch],
        flops,
        pixels * channels * 8,
        "states",
    )(frame_step, bits[0], rate, after(incoming, backward.message), far(driven), far(cotangent))

    def conv(value, kernel_map, reverse, base, size, previous=None):
        specs = [framed(shape, block, size, False, base), fixed(weights)]
        operands = [far(value), kernel_map]
        aliases = {}
        if previous is not None:
            specs.append(pl.BlockSpec(memory_space=pl.ANY))
            operands.append(previous)
            aliases = {2: 0}
        return call(
            functools.partial(conv_kernel, reverse),
            (size,),
            specs,
            framed(shape, block, size, False, base),
            low_type,
            [flip_scratch],
            flops * size // steps,
            pixels * channels * 4 * size // steps,
            "conv",
            aliases,
        )(*operands)

    orders = (list(range(levels)), [0, 2, 1] + list(range(3, levels)))
    backward.combine_rest(out_send)
    arriving = backward.result()
    out_sum = Sum(out_keep, out_send, bits, orders, count, grad_rows)
    out_sum.start()
    out_sum.step()

    adjoint_low, in_keep, in_send = call(
        functools.partial(adjoint_kernel, factor, steps - later),
        grid,
        [
            smem(),
            smem(),
            fixed(rate.shape),
            fixed(incoming.shape),
            fixed(incoming.shape),
            pl.BlockSpec((block,) + shape[1:], lambda g: (jnp.maximum(steps - 1 - g - later, 0), 0, 0, 0)),
            pl.BlockSpec((block,) + shape[1:], lambda g: (jnp.minimum(steps - 1 - g, later - 1), 0, 0, 0)),
            framed(shape, block, steps, True),
            framed(shape, block, steps, True),
            pl.BlockSpec((1,) + shape[1:], lambda g: (jnp.maximum((steps - 1 - g) * block - 1, 0), 0, 0, 0)),
        ],
        [framed(shape, block, steps, True), fixed(padded_type.shape), fixed(padded_type.shape)],
        [low_type, padded_type, padded_type],
        [map_scratch, decay_scratch, sums_scratch, pltpu.VMEM((padded_rows, channels), F32)],
        flops,
        pixels * channels * 10,
        "adjoint",
    )(
        frame_step,
        bits[0],
        rate,
        after(arriving, out_sum.send),
        incoming,
        far(pulled_late),
        far(pulled_early),
        far(latents),
        far(states_low),
        far(states_low),
    )

    out_sum.wait(in_send)
    out_sum.step()
    in_sum = Sum(in_keep, after(in_send, out_sum.send), bits, orders, count, grad_rows)
    in_sum.start()
    covers = [(adjoint_low, input_map, True), (states_low, output_map, False)]
    convs = []
    latest = out_sum.send
    for turn in turns(levels):
        if turn == "c":
            value, kernel_map, reverse = covers.pop()
            convs.append(conv(after(value, latest), kernel_map, reverse, 0, steps))
            latest = convs[-1]
        else:
            one = out_sum if turn == "o" else in_sum
            one.wait(latest)
            one.step()
            latest = one.send
    layer_out, grad_latents = convs
    grad_output_map, (grad_input_map, rate_rows) = out_sum.send, in_sum.send
    grad_log_rate = -factor * decay_rate * jnp.sum(rate_rows, axis=0)
    return (
        layer_out,
        grad_latents,
        grad_input_map.reshape(weights),
        grad_output_map.reshape(weights),
        grad_log_rate,
    )


def solution(mesh):
    in_specs = (
        P(("groups", "tm"), None, None, None),
        P(),
        P(),
        P(),
        P(("groups", "tm")),
        P(("groups", "tm"), None, None, None),
    )
    out_specs = (
        P(("groups", "tm"), None, None, None),
        P(("groups", "tm"), None, None, None),
        P("groups", None, None),
        P("groups", None, None),
        P("groups"),
    )
    return jax.shard_map(body, mesh=mesh, in_specs=in_specs, out_specs=out_specs, check_vma=False)
```

```python
import functools
import math

import jax
import jax.numpy as jnp
from jax import lax
from jax.experimental import pallas as pl
from jax.experimental.pallas import tpu as pltpu
from jax.sharding import PartitionSpec as P

F32 = jnp.float32
BF16 = jnp.bfloat16
VMEM_LIMIT = 36 * 1024 * 1024


def column_shifts(value):
    frames, height, breadth, channels = value.shape
    rows = frames * height * breadth
    flat = value.reshape(rows, channels).astype(F32)
    column = lax.broadcasted_iota(jnp.int32, (rows, channels), 0) % breadth
    before = jnp.where(column == 0, 0.0, pltpu.roll(flat, 1, 0)).astype(BF16)
    after = jnp.where(column == breadth - 1, 0.0, pltpu.roll(flat, rows - 1, 0)).astype(BF16)
    return before.reshape(value.shape), value, after.reshape(value.shape)


def conv_rows(value, weights):
    frames, _, breadth, channels = value.shape
    shifted = column_shifts(value)
    pieces = [piece[:, row].reshape(frames * breadth, channels) for row in (0, 1) for piece in shifted]
    patches = jnp.concatenate(pieces, axis=1)
    outs = []
    for first in (3, 0):
        taps = weights[first : first + 6].reshape(6 * channels, weights.shape[2])
        outs.append(jnp.dot(patches, taps, preferred_element_type=F32))
    return outs


def flip_into(flipped_ref, weights_ref):
    for tap in range(9):
        flipped_ref[tap] = weights_ref[8 - tap].T


def decay_of(step, rate):
    return jnp.exp(-(step * rate))


def drive_kernel(reverse, base, fresh, step_ref, rate_ref, value_ref, weights_ref, *refs):
    start_ref, refs = (None, refs) if fresh else (refs[0], refs[1:])
    driven_ref, carry_ref, state, decay, flipped = refs
    index, count = pl.program_id(0), pl.num_programs(0)
    block, _, breadth, channels = driven_ref.shape
    map_rows = state.shape[0] * 8

    @pl.when(index == 0)
    def _():
        state[...] = jnp.zeros_like(state) if fresh else start_ref[:map_rows].reshape(state.shape)
        decay[...] = jnp.ones_like(decay) if fresh else start_ref[map_rows:]
        if reverse:
            flip_into(flipped, weights_ref)

    outs = conv_rows(value_ref[...], flipped if reverse else weights_ref)
    for row, out in enumerate(outs):
        driven_ref[:, row] = out.reshape(block, breadth, channels)
    first = (base + (count - 1 - index if reverse else index)) * block
    rate = jnp.broadcast_to(rate_ref[...], decay.shape)
    total, held = decay[...], state[...]
    for offset in range(block):
        frame = block - 1 - offset if reverse else offset
        factor = decay_of(step_ref[first + frame], rate)
        driven = driven_ref[frame].reshape(state.shape)
        held = factor[None] * (held + driven) if reverse else factor[None] * held + driven
        total = total * factor
    state[...] = held
    decay[...] = total

    @pl.when(index == count - 1)
    def _():
        carry_ref[:map_rows] = held.reshape(map_rows, channels)
        carry_ref[map_rows:] = total


def add_kernel_grad(sums, source, target):
    frames, height, breadth, channels = source.shape
    before, same, after = column_shifts(target)
    taps = jnp.concatenate([after, same, before], axis=-1)

    def contract(left, right):
        return lax.dot_general(
            left.reshape(-1, channels), right.reshape(-1, 3 * channels), (((0,), (0,)), ((), ())), preferred_element_type=F32
        )

    sums[1] += contract(source, taps)
    sums[0] += contract(source[:, 0], taps[:, 1])
    sums[2] += contract(source[:, 1], taps[:, 0])


def split_grad(scale, sums, whole, core, keep_ref, send_ref, rate_sum=None):
    channels = sums.shape[1]
    rows = 9 * channels
    if rate_sum is not None:
        whole[rows:] = jnp.zeros((whole.shape[0] - rows, channels), F32)
        whole[rows : rows + 8] = rate_sum
    for tap in range(9):
        piece = sums[tap // 3, :, (tap % 3) * channels : (tap % 3 + 1) * channels]
        whole[tap * channels : (tap + 1) * channels] = piece * scale
    half = whole.shape[0] // 2
    keep_ref[...] = whole[pl.ds(core * half, half)]
    send_ref[...] = whole[pl.ds((1 - core) * half, half)]


def state_kernel(
    scale, step_ref, core_ref, rate_ref, incoming_ref, driven_ref, cotangent_ref, low_ref, keep_ref, send_ref, state, sums, whole
):
    index, count = pl.program_id(0), pl.num_programs(0)
    block = driven_ref.shape[0]

    @pl.when(index == 0)
    def _():
        state[...] = incoming_ref[...].reshape(state.shape)
        sums[...] = jnp.zeros_like(sums)

    rate = jnp.broadcast_to(rate_ref[...], (8, rate_ref.shape[1]))
    held = state[...]
    for frame in range(block):
        factor = decay_of(step_ref[index * block + frame], rate)
        held = factor[None] * held + driven_ref[frame].reshape(state.shape)
        low_ref[frame] = held.astype(BF16).reshape(low_ref.shape[1:])
    state[...] = held
    add_kernel_grad(sums, low_ref[...], cotangent_ref[...])

    @pl.when(index == count - 1)
    def _():
        split_grad(scale, sums, whole, core_ref[0], keep_ref, send_ref)


def adjoint_kernel(
    scale,
    late_steps,
    step_ref,
    core_ref,
    rate_ref,
    arriving_ref,
    incoming_ref,
    late_ref,
    early_ref,
    latents_ref,
    states_ref,
    previous_ref,
    low_ref,
    keep_ref,
    send_ref,
    carry,
    rate_sum,
    sums,
    whole,
):
    index, count = pl.program_id(0), pl.num_programs(0)
    block = late_ref.shape[0]
    first = (count - 1 - index) * block

    @pl.when(index == 0)
    def _():
        carry[...] = arriving_ref[...].reshape(carry.shape)
        rate_sum[...] = jnp.zeros_like(rate_sum)
        sums[...] = jnp.zeros_like(sums)

    rate = jnp.broadcast_to(rate_ref[...], rate_sum.shape)
    held, summed = carry[...], rate_sum[...]
    for frame in range(block - 1, -1, -1):
        step = step_ref[first + frame]
        pulled = jnp.where(index < late_steps, late_ref[frame], early_ref[frame])
        adjoint = held + pulled.reshape(carry.shape)
        low_ref[frame] = adjoint.astype(BF16).reshape(low_ref.shape[1:])
        held = decay_of(step, rate)[None] * adjoint
        if frame:
            before = states_ref[frame - 1].astype(F32).reshape(carry.shape)
        else:
            before = jnp.where(
                index == count - 1,
                incoming_ref[...].reshape(carry.shape),
                previous_ref[0].astype(F32).reshape(carry.shape),
            )
        summed = summed + step * jnp.sum(held * before, axis=0)
    carry[...] = held
    rate_sum[...] = summed
    add_kernel_grad(sums, latents_ref[...], low_ref[...])

    @pl.when(index == count - 1)
    def _():
        split_grad(scale, sums, whole, core_ref[0], keep_ref, send_ref, summed)


def conv_kernel(reverse, value_ref, weights_ref, *refs):
    out_ref, flipped = refs[-2:]
    if reverse:

        @pl.when(pl.program_id(0) == 0)
        def _():
            flip_into(flipped, weights_ref)

    block, _, breadth, channels = out_ref.shape
    outs = conv_rows(value_ref[...], flipped if reverse else weights_ref)
    for row, out in enumerate(outs):
        out_ref[:, row] = out.astype(BF16).reshape(block, breadth, channels)


def call(kernel, grid, in_specs, out_specs, out_shape, scratch, flops, moved, name, aliases=None):
    return pl.pallas_call(
        kernel,
        grid=grid,
        in_specs=in_specs,
        out_specs=out_specs,
        out_shape=out_shape,
        scratch_shapes=scratch,
        input_output_aliases=aliases or {},
        compiler_params=pltpu.CompilerParams(vmem_limit_bytes=VMEM_LIMIT, dimension_semantics=("arbitrary",) * len(grid)),
        cost_estimate=pl.CostEstimate(flops=flops, bytes_accessed=moved, transcendentals=0),
        name=name,
    )


def far(value):
    return pltpu.with_memory_space_constraint(value, pltpu.HBM)


def smem():
    return pl.BlockSpec(memory_space=pltpu.SMEM)


def fixed(shape):
    return pl.BlockSpec(shape, lambda g: (0,) * len(shape))


def framed(shape, block, count, reverse, base=0):
    return pl.BlockSpec((block,) + shape[1:], lambda g: (base + (count - 1 - g if reverse else g), 0, 0, 0))


def part_of(bit, value):
    half = value.shape[0] // 2
    return lax.dynamic_slice_in_dim(value, bit[0] * half, half)


def merge(bit, mine, other, rows=None):
    if rows is None or rows == 2 * mine.shape[0]:
        return jnp.where(bit[0] == 0, jnp.concatenate([mine, other]), jnp.concatenate([other, mine]))
    cut = rows - mine.shape[0]
    first, last = (mine, other[: cut + 8]), (other, mine[: cut + 8])
    main = jnp.where(bit[0] == 0, jnp.concatenate([first[0], first[1][:cut]]), jnp.concatenate([last[0], last[1][:cut]]))
    return main, jnp.where(bit[0] == 0, first[1][cut:], last[1][cut:])


def swap(value, count, distance):
    return lax.ppermute(value, "tm", [(source, source ^ distance) for source in range(count)])


def bits_of(me, levels):
    return [jnp.bitwise_and(lax.shift_right_logical(me, level), 1).reshape(1) for level in range(levels)]


def after(value, *others):
    return lax.optimization_barrier((value, *others))[0]


class Sum:
    def __init__(self, keep, send, bits, orders, count, rows):
        self.keep, self.send, self.count, self.rows = keep, send, count, rows
        self.orders = orders
        self.bits = [jnp.where(bits[0] == 0, bits[even], bits[odd]) for even, odd in zip(*orders)]
        self.stage = 0
        self.left = 2 * len(self.bits)

    def swap(self, value):
        levels = [order[self.stage] for order in self.orders]
        return lax.ppermute(value, "tm", [(source, source ^ (1 << levels[source & 1])) for source in range(self.count)])

    def start(self):
        self.recv = self.swap(self.send)

    def wait(self, *others):
        self.recv = after(self.recv, *others)

    def fold(self):
        total = self.keep + self.recv
        self.stage += 1
        if self.stage == len(self.bits):
            self.send = total
            return
        bit = self.bits[self.stage]
        self.keep, self.send = part_of(bit, total), part_of(1 - bit, total)

    def step(self):
        if self.left == 0:
            return
        if self.left > len(self.bits):
            self.fold()
        else:
            self.send = merge(self.bits[self.stage], self.send, self.recv, self.rows if self.left == 1 else None)
        self.left -= 1
        if self.left > len(self.bits):
            self.start()
        elif self.left:
            self.stage -= 1
            self.start()


class Carry:
    def __init__(self, message, bits, count, reverse):
        self.message, self.bits, self.count, self.reverse = message, bits, count, reverse
        self.rows = message.shape[0] - 8
        self.reached = jnp.zeros((self.rows // 8, 8, message.shape[1]), F32)
        self.passed = jnp.ones((1, 8, message.shape[1]), F32)
        self.level = 0

    def split(self, message):
        return message[: self.rows].reshape(self.reached.shape), message[self.rows :][None]

    def start(self):
        distance = 1 << self.level
        pairs = [(source, source ^ distance) for source in range(self.count)]
        if self.level == len(self.bits) - 1:
            towards = 0 if self.reverse else distance
            pairs = [pair for pair in pairs if pair[1] & distance == towards]
        self.other = lax.ppermute(self.message, "tm", pairs)

    def combine(self, *others):
        self.other = after(self.other, *others)
        (local, decay), (other_local, other_decay) = self.split(self.message), self.split(self.other)
        later = self.bits[self.level][0] == (0 if self.reverse else 1)
        self.reached = jnp.where(later, self.reached + self.passed * other_local, self.reached)
        self.passed = jnp.where(later, self.passed * other_decay, self.passed)
        local = jnp.where(later, decay * other_local + local, other_decay * local + other_local)
        self.level += 1
        self.message = jnp.concatenate([local.reshape(self.rows, -1), (decay * other_decay)[0]], axis=0)

    def start_rest(self):
        runs = self.count // 4
        hops = [-4 * hop if self.reverse else 4 * hop for hop in range(1, runs)]
        self.rest = [
            lax.ppermute(
                self.message, "tm", [(source, source + hop) for source in range(self.count) if 0 <= source + hop < self.count]
            )
            for hop in hops
        ]

    def combine_rest(self, *others):
        held = jnp.zeros_like(self.reached)
        for message in self.rest[::-1]:
            local, decay = self.split(after(message, *others))
            held = local + decay * held
        self.reached = self.reached + self.passed * held

    def result(self):
        return self.reached.reshape(self.rows, -1)


def turns(levels):
    return "icoioioc" + "io" * (2 * levels - 5) + "ii"


def body(latents, input_map, output_map, decay_rate, frame_step, cotangent):
    frames, height, breadth, channels = latents.shape
    count = lax.axis_size("tm")
    levels = count.bit_length() - 1
    me = lax.axis_index("tm")
    bits = bits_of(me, levels)
    factor = 1.0 / math.sqrt(frames * count * height * breadth)
    block = 32
    steps = frames // block
    grid = (steps,)
    rate = decay_rate.reshape(1, channels)
    map_rows = height * breadth
    shape = latents.shape
    weights = input_map.shape
    pixels = frames * height * breadth
    flops = 2 * pixels * 6 * channels * channels
    driven_type = pltpu.HBM(shape, F32)
    low_type = pltpu.HBM(shape, BF16)
    map_scratch = pltpu.VMEM((map_rows // 8, 8, channels), F32)
    decay_scratch = pltpu.VMEM((8, channels), F32)
    flip_scratch = pltpu.VMEM(weights, BF16)

    def drive(value, kernel_map, reverse, base, size, start=None):
        specs = [smem(), fixed(rate.shape), framed(shape, block, size, reverse, base), fixed(weights)]
        operands = [far(frame_step), far(rate), far(value), kernel_map if reverse else far(kernel_map)]
        if start is not None:
            specs.append(fixed((map_rows + 8, channels)))
            operands.append(start)
        return call(
            functools.partial(drive_kernel, reverse, base, start is None),
            (size,),
            specs,
            [framed(shape, block, size, reverse), fixed((map_rows + 8, channels))],
            [pltpu.HBM((size * block,) + shape[1:], F32), jax.ShapeDtypeStruct((map_rows + 8, channels), F32)],
            [map_scratch, decay_scratch, flip_scratch],
            flops * size // steps,
            pixels * channels * 6 * size // steps,
            "pull" if reverse else "drive",
        )(*operands)

    driven, forward_carry = drive(latents, input_map, False, 0, steps)
    forward = Carry(forward_carry, bits, count, False)
    forward.start()
    later = steps // 2
    pulled_late, late_carry = drive(after(cotangent, forward_carry), output_map, True, later, steps - later)
    forward.combine(late_carry)
    forward.start()
    pulled_early, backward_carry = drive(cotangent, output_map, True, 0, later, after(late_carry, forward.message))
    forward.combine(backward_carry)
    forward.start()
    backward = Carry(after(backward_carry, forward.message), bits, count, True)
    backward.start()
    for _ in range(levels - 3):
        forward.combine()
        forward.start()
        if backward.level == 0:
            backward.combine(forward.message)
            backward.start()
    forward.combine()
    incoming = forward.result()
    backward.combine(incoming)
    backward.start_rest()

    grad_rows = 9 * channels
    half = grad_rows // 2
    sums_scratch = pltpu.VMEM((3, channels, 3 * channels), F32)
    whole_scratch = pltpu.VMEM((grad_rows, channels), F32)
    half_type = jax.ShapeDtypeStruct((half, channels), F32)
    padded_rows = grad_rows + 8 * count
    padded_type = jax.ShapeDtypeStruct((padded_rows // 2, channels), F32)

    states_low, out_keep, out_send = call(
        functools.partial(state_kernel, factor),
        grid,
        [
            smem(),
            smem(),
            fixed(rate.shape),
            fixed(incoming.shape),
            framed(shape, block, steps, False),
            framed(shape, block, steps, False),
        ],
        [framed(shape, block, steps, False), fixed(half_type.shape), fixed(half_type.shape)],
        [low_type, half_type, half_type],
        [map_scratch, sums_scratch, whole_scratch],
        flops,
        pixels * channels * 8,
        "states",
    )(frame_step, bits[0], rate, after(incoming, backward.message), far(driven), far(cotangent))

    def conv(value, kernel_map, reverse, base, size, previous=None):
        specs = [framed(shape, block, size, False, base), fixed(weights)]
        operands = [far(value), kernel_map]
        aliases = {}
        if previous is not None:
            specs.append(pl.BlockSpec(memory_space=pl.ANY))
            operands.append(previous)
            aliases = {2: 0}
        return call(
            functools.partial(conv_kernel, reverse),
            (size,),
            specs,
            framed(shape, block, size, False, base),
            low_type,
            [flip_scratch],
            flops * size // steps,
            pixels * channels * 4 * size // steps,
            "conv",
            aliases,
        )(*operands)

    orders = (list(range(levels)), [0, 2, 1] + list(range(3, levels)))
    backward.combine_rest(out_send)
    arriving = backward.result()
    out_sum = Sum(out_keep, out_send, bits, orders, count, grad_rows)
    out_sum.start()
    out_sum.step()

    adjoint_low, in_keep, in_send = call(
        functools.partial(adjoint_kernel, factor, steps - later),
        grid,
        [
            smem(),
            smem(),
            fixed(rate.shape),
            fixed(incoming.shape),
            fixed(incoming.shape),
            pl.BlockSpec((block,) + shape[1:], lambda g: (jnp.maximum(steps - 1 - g - later, 0), 0, 0, 0)),
            pl.BlockSpec((block,) + shape[1:], lambda g: (jnp.minimum(steps - 1 - g, later - 1), 0, 0, 0)),
            framed(shape, block, steps, True),
            framed(shape, block, steps, True),
            pl.BlockSpec((1,) + shape[1:], lambda g: (jnp.maximum((steps - 1 - g) * block - 1, 0), 0, 0, 0)),
        ],
        [framed(shape, block, steps, True), fixed(padded_type.shape), fixed(padded_type.shape)],
        [low_type, padded_type, padded_type],
        [map_scratch, decay_scratch, sums_scratch, pltpu.VMEM((padded_rows, channels), F32)],
        flops,
        pixels * channels * 10,
        "adjoint",
    )(
        frame_step,
        bits[0],
        rate,
        after(arriving, out_sum.send),
        incoming,
        far(pulled_late),
        far(pulled_early),
        far(latents),
        far(states_low),
        far(states_low),
    )

    out_sum.wait(in_send)
    out_sum.step()
    in_sum = Sum(in_keep, after(in_send, out_sum.send), bits, orders, count, grad_rows)
    in_sum.start()
    covers = [(adjoint_low, input_map, True), (states_low, output_map, False)]
    convs = []
    latest = out_sum.send
    for turn in turns(levels):
        if turn == "c":
            value, kernel_map, reverse = covers.pop()
            convs.append(conv(after(value, latest), kernel_map, reverse, 0, steps))
            latest = convs[-1]
        else:
            one = out_sum if turn == "o" else in_sum
            one.wait(latest)
            one.step()
            latest = one.send
    layer_out, grad_latents = convs
    grad_output_map, (grad_input_map, rate_rows) = out_sum.send, in_sum.send
    grad_log_rate = -factor * decay_rate * jnp.sum(rate_rows, axis=0)
    return (
        layer_out,
        grad_latents,
        grad_input_map.reshape(weights),
        grad_output_map.reshape(weights),
        grad_log_rate,
    )


def solution(mesh):
    in_specs = (
        P(("groups", "tm"), None, None, None),
        P(),
        P(),
        P(),
        P(("groups", "tm")),
        P(("groups", "tm"), None, None, None),
    )
    out_specs = (
        P(("groups", "tm"), None, None, None),
        P(("groups", "tm"), None, None, None),
        P("groups", None, None),
        P("groups", None, None),
        P("groups"),
    )
    return jax.shard_map(body, mesh=mesh, in_specs=in_specs, out_specs=out_specs, check_vma=False)
```
